1024 devices in a mesh: group: 8 (over x, z_hi), tp: 16 (over z_lo), dp: 8 (over y, core).
Axes of the slice: x: 4, y: 4, z: 32 (z_hi: 2, z_lo: 16; z = z_hi * 16 + z_lo), core: 2. Of those that a mesh axis runs over, the one named last changes fastest.
Arguments:
- image_slots: bfloat16 [2048, 8192], P(('group', 'tp'), 'dp'), may hold values from -6 to 6
- image_cot: bfloat16 [2048, 8192], P(('group', 'tp'), 'dp'), may hold values from -6 to 6
- text_rows: bfloat16 [1024, 8192], P(('group', 'tp'), 'dp'), may hold values from -6 to 6
- text_cot: bfloat16 [1024, 8192], P(('group', 'tp'), 'dp'), may hold values from -6 to 6
- destination: int32 [1024, 1], P(('group', 'tp')), may hold values from 0 to 7; in each aligned block of 8 rows (0 to 7, 8 to 15, ...) at most 2 rows name the same one
- text_count: int32 [128], P(('group', 'tp')), may hold values from 1 to 8, 768 in all
- w_gate: bfloat16 [8192, 14336], P('dp', 'tp'), may hold values from -0.0625 to 0.0625
- w_up: bfloat16 [8192, 14336], P('dp', 'tp'), may hold values from -0.0625 to 0.0625
- w_down: bfloat16 [14336, 8192], P('tp', 'dp'), may hold values from -0.046875 to 0.046875
Outputs:
- image_grad: bfloat16 [1024, 8192], P(('group', 'tp'), 'dp')
- text_grad: bfloat16 [1024, 8192], P(('group', 'tp'), 'dp')
The draws below stay inside these ranges and needn't reach their ends.
Inputs may be any that keep to these rules, and one draw needn't show every extreme that they name: In the rows of one block of 8 rows no group is named more than 2 times, and some block names one group exactly 2 times; destination[i] decides which slot of image_slots and image_cot holds row i. Each block of 8 text rows has text_count live rows first; some block is full.
All inputs are finite; a program needn't handle non-finite values.
Results may differ from the reference program's by a relative error of at most 0.025.
Values may be sent and summed in bfloat16 or wider, within the bound.
A program may use at most 32 MiB of HBM per device.

```python
import math
import jax
import jax.numpy as jnp
import numpy as np
from jax import lax

D = 8192
FF = 14336
IMG_DEV = 8
TXT_DEV = 8
CAP = 2
SLOTS = 2048
IMG_ROWS = 1024
TXT_ROWS = 1024
N_GROUP = 8
N_TP = 16
N_DP = 8


def block_scale(stream_key, shape, cuts, least, high):
    factor_of = 1.0
    for dim, blocks in cuts:
        steps = jax.random.uniform(jax.random.fold_in(jax.random.fold_in(stream_key, 6), dim), (blocks,), jnp.float32, least / len(cuts), high / len(cuts))
        factor_of = factor_of * jnp.repeat(jnp.exp(steps), shape[dim] // blocks).reshape((-1,) + (1,) * (len(shape) - 1 - dim))
    return factor_of


def split_up(amount, total, most, slope):
    portions = [(1 << 20) // math.isqrt(grade ** slope) + 1 for grade in range(2, amount + 1)]
    surplus, given = total - most - (amount - 1), [1] * (amount - 1)
    while surplus > 0:
        movable = [i for i in range(amount - 1) if given[i] < most]
        whole, left = sum([portions[i] for i in movable]), surplus
        for i in movable:
            extra = min(most - given[i], max(1, left * portions[i] // whole), surplus)
            given[i] = given[i] + extra
            surplus = surplus - extra
    return np.array([most] + given)


def ragged(stream_key, count, total, most, slope):
    if count == 2:
        one = jax.random.randint(stream_key, (), max(1, total - most), min(most, total - 1) + 1)
        return jnp.stack([one, total - one])
    sizes = jnp.asarray(split_up(count, total, most, slope), jnp.int32)
    couples = (count - 1) // 2
    donor, taker = sizes[1:1 + 2 * couples:2], sizes[2:2 + 2 * couples:2]
    slack = jnp.minimum(donor - 1, most - taker)
    shifted = jax.random.randint(jax.random.fold_in(stream_key, 1), (couples,), 0, 1 << 20) % (slack + 1)
    sizes = sizes.at[1:1 + 2 * couples:2].set(donor - shifted).at[2:2 + 2 * couples:2].set(taker + shifted)
    return sizes[jax.random.permutation(jax.random.fold_in(stream_key, 2), count)]


def shared_out(rng, own, number, rows, number_of, top, bound, lean):
    sequence = jax.random.permutation(rng, number_of)
    packed, usual = load_shares(number_of, rows * top, bound, lean, True), load_shares(number_of, rows * top, bound, lean, False)
    places = jnp.arange(number_of)

    def named(tallies, rotation):
        used = int((tallies > 0).sum())
        fixed = max(1, used // 4)
        shifted = fixed + (places - fixed + rotation * (used - fixed)) % max(1, number_of - fixed)
        return jnp.zeros((number_of,), jnp.int32).at[sequence[jnp.where(places < fixed, places, shifted)]].set(jnp.asarray(tallies, jnp.int32))

    tallies = jnp.where(number % 4 == 0, named(packed, number // 4), named(usual, number - number // 4 - 1))
    mixed = jax.random.permutation(jax.random.fold_in(own, 3), number_of)
    source_of, receiver = mixed[0:number_of // 2 * 2:2], mixed[1:number_of // 2 * 2:2]
    margin = jnp.minimum(tallies[source_of] - 1, bound - tallies[receiver]) // 2
    margin = jnp.where((source_of == sequence[0]) | (receiver == sequence[0]) | (tallies[receiver] == 0), 0, jnp.maximum(margin, 0))
    shifted = jax.random.randint(jax.random.fold_in(own, 4), (number_of // 2,), 0, 1 << 20) % (margin + 1)
    tallies = tallies.at[source_of].add(-shifted).at[receiver].add(shifted)
    labels = jnp.searchsorted(jnp.cumsum(tallies), jnp.arange(rows * top), side="right").astype(jnp.int32)
    grid = labels.reshape(top, rows).T
    grid = grid[jax.random.permutation(jax.random.fold_in(own, 1), rows)]
    rotation = jax.random.randint(jax.random.fold_in(own, 2), (rows, 1), 0, top)
    return jnp.take_along_axis(grid, (jnp.arange(top)[None, :] + rotation) % top, axis=1)


def load_shares(number_of, total, most, skew, full):
    weights = [(1 << 20) // math.isqrt(grade ** skew) + 1 for grade in range(1, number_of + 1)]
    largest = most if full else min(most, max(-(-total // number_of), total * weights[0] // sum(weights)))
    least = 1 if total - largest >= number_of - 1 else 0
    given, spare = [largest] + [least] * (number_of - 1), total - largest - least * (number_of - 1)
    while spare > 0:
        movable = [i for i in range(1, number_of) if given[i] < largest] or [i for i in range(1, number_of) if given[i] < most]
        pool, budget = sum([weights[i] for i in movable]), spare
        for i in movable:
            addition = min(most - given[i], max(1, budget * weights[i] // pool), spare)
            given[i] = given[i] + addition
            spare = spare - addition
    return np.array(given)


def centred(key, extent, deviation, reach, pieces=(), kind=jnp.bfloat16):
    drawn = deviation * jax.random.normal(key, extent, jnp.float32)
    if pieces:
        drawn = drawn * block_scale(key, extent, pieces, -0.22, 0.18)
    return jnp.clip(drawn, -reach, reach).astype(kind)


def setup_inputs(seed: int = 0) -> dict:
    streams_of = jax.random.split(jax.random.key(seed), 10)
    image_slots = centred(streams_of[0], (SLOTS, D), 1.0, 6.0, ((0, 128), (1, 8)))
    image_cot = centred(streams_of[1], (SLOTS, D), 1.0, 6.0, ((0, 128), (1, 8)))
    text_rows = centred(streams_of[2], (TXT_ROWS, D), 1.0, 6.0, ((0, 128), (1, 8)))
    text_cot = centred(streams_of[3], (TXT_ROWS, D), 1.0, 6.0, ((0, 128), (1, 8)))
    destination_keys = jax.random.split(jax.random.fold_in(streams_of[4], 1), IMG_ROWS // IMG_DEV)
    destination_turns = jax.random.permutation(jax.random.fold_in(streams_of[4], 3), IMG_ROWS // IMG_DEV)
    destination = jax.vmap(lambda own, number: shared_out(jax.random.fold_in(streams_of[4], 2), own, number, IMG_DEV, N_GROUP, 1, CAP, 2))(destination_keys, destination_turns).reshape((IMG_ROWS, 1))
    text_count = ragged(streams_of[5], N_GROUP * N_TP, 3 * TXT_DEV * N_GROUP * N_TP // 4, TXT_DEV, 2).astype(jnp.int32)
    w_gate = centred(streams_of[6], (D, FF), D ** -0.5, 0.0625, ((0, 8), (1, 16)))
    w_up = centred(streams_of[7], (D, FF), D ** -0.5, 0.0625, ((0, 8), (1, 16)))
    w_down = centred(streams_of[8], (FF, D), FF ** -0.5, 0.046875, ((0, 16), (1, 8)))
    return {"image_slots": image_slots, "image_cot": image_cot, "text_rows": text_rows, "text_cot": text_cot, "destination": destination, "text_count": text_count, "w_gate": w_gate, "w_up": w_up, "w_down": w_down}


def rounded(value):
    return lax.optimization_barrier(value.astype(jnp.bfloat16)).astype(jnp.float32)


def split_features(left, right, parts, transpose_right):
    width = left.shape[1] // parts
    if transpose_right:
        total = jnp.zeros((left.shape[0], right.shape[0]), jnp.float32)
    else:
        total = jnp.zeros((left.shape[0], right.shape[1]), jnp.float32)

    def add_block(index, carry):
        start = (index * width).astype(jnp.int32)
        piece = lax.dynamic_slice_in_dim(left, start, width, 1)
        if transpose_right:
            other = lax.dynamic_slice_in_dim(right, start, width, 1)
            term = lax.dot_general(piece, other, (((1,), (1,)), ((), ())), preferred_element_type=jnp.float32)
        else:
            other = lax.dynamic_slice_in_dim(right, start, width, 0)
            term = jnp.dot(piece, other, preferred_element_type=jnp.float32)
        return carry + rounded(term)

    return lax.fori_loop(0, parts, add_block, total)


def split_hidden(dgate, dup, w_gate, w_up, parts):
    width = dgate.shape[1] // parts
    total = jnp.zeros((dgate.shape[0], w_gate.shape[0]), jnp.float32)

    def add_block(index, carry):
        start = (index * width).astype(jnp.int32)
        gate_piece = lax.dynamic_slice_in_dim(dgate, start, width, 1)
        up_piece = lax.dynamic_slice_in_dim(dup, start, width, 1)
        gate_weight = lax.dynamic_slice_in_dim(w_gate, start, width, 1)
        up_weight = lax.dynamic_slice_in_dim(w_up, start, width, 1)
        term = lax.dot_general(gate_piece, gate_weight, (((1,), (1,)), ((), ())), preferred_element_type=jnp.float32)
        term = term + lax.dot_general(up_piece, up_weight, (((1,), (1,)), ((), ())), preferred_element_type=jnp.float32)
        return carry + rounded(term)

    return lax.fori_loop(0, parts, add_block, total)


def row_grads(rows, cots, w_gate, w_up, w_down):
    gate = split_features(rows, w_gate, N_DP, False)
    up = split_features(rows, w_up, N_DP, False)
    back = split_features(cots, w_down, N_DP, True)
    sigmoid_gate = jax.nn.sigmoid(gate)
    dgate = (back * up * sigmoid_gate * (1.0 + gate * (1.0 - sigmoid_gate))).astype(jnp.bfloat16)
    dup = (back * gate * sigmoid_gate).astype(jnp.bfloat16)
    total = split_hidden(dgate, dup, w_gate, w_up, N_TP)
    return total.astype(jnp.bfloat16)


def reference(image_slots, image_cot, text_rows, text_cot, destination, text_count, w_gate, w_up, w_down):
    blocks = destination[:, 0].astype(jnp.int32).reshape(N_GROUP * N_TP, IMG_DEV)
    same = blocks[:, :, None] == blocks[:, None, :]
    position = jnp.arange(IMG_DEV, dtype=jnp.int32)
    earlier = position[None, :] < position[:, None]
    rank = jnp.sum((same & earlier[None, :, :]).astype(jnp.int32), axis=2)
    source = jnp.arange(N_GROUP * N_TP, dtype=jnp.int32)
    source_group = source // N_TP
    source_tp = source % N_TP
    slot = ((blocks * N_TP + source_tp[:, None]) * N_GROUP + source_group[:, None]) * CAP + rank
    slot = slot.reshape(-1).astype(jnp.int32)
    image_in = jnp.take(image_slots, slot, axis=0)
    image_back = jnp.take(image_cot, slot, axis=0)
    image_grad = row_grads(image_in, image_back, w_gate, w_up, w_down)
    text_grad = row_grads(text_rows, text_cot, w_gate, w_up, w_down)
    within = jnp.arange(TXT_ROWS, dtype=jnp.int32) % TXT_DEV
    limit = jnp.repeat(text_count.astype(jnp.int32), TXT_DEV)
    live = (within < limit)[:, None]
    text_grad = jnp.where(live, text_grad, jnp.zeros_like(text_grad))
    return image_grad, text_grad
```

```python
import functools

import jax
import jax.numpy as jnp
from jax import lax
from jax.experimental import pallas as pl
from jax.experimental.pallas import tpu as pltpu
from jax.sharding import PartitionSpec as P

MESH = pl.DeviceIdType.MESH
F32 = jnp.float32
BF16 = jnp.bfloat16
ROWS = 8
KINDS = 3


def kernel(
    nx, nt, ny, cap, feat, hid,
    cand_ref, text_ref, col_ref, live_ref, wg_ref, wu_ref, wd_ref,
    img_ref, txt_ref,
    wg, wu, wd, xr, mix, tb, ib, xs, cs, part, mate, summed, parts_in, grads, ds, terms,
    ra_l, ra_r, sa_l, sa_r, far_a, far_a_in,
    rn_l, rn_r, sn_l, sn_r, rf_l, rf_r, sf_l, sf_r,
    wsem, xs_s, xs_r, hop_s, hop_r, mate_s, mate_r, y_s, y_r, ag_s, ag_r, fw_s, fw_r,
    a_s, a_r, b_s, b_r, f_s, f_r,
):
    ring = 2 * nt
    right_hops, left_hops = nt // 2, nt // 2 - 1
    half = nt // 4
    own = right_hops
    g, t, d = lax.axis_index("group"), lax.axis_index("tp"), lax.axis_index("dp")
    x, z, y, c = g // 2, (g % 2) * nt + t, d // 2, d % 2

    def at(dx=0, dz=0, dy=0, flip=False):
        zz = lax.rem(z + dz + ring, ring)
        xx = lax.rem(x + dx, nx)
        yy = lax.rem(y + dy, ny)
        cc = 1 - c if flip else c
        return {"group": xx * 2 + zz // nt, "tp": lax.rem(zz, nt), "dp": yy * 2 + cc}

    started = []

    def send(src, dst, s, r, device):
        copy = pltpu.make_async_remote_copy(
            src, dst, s, r, device_id=device, device_id_type=MESH
        )
        copy.start()
        started.append(copy)
        return copy

    loads = [
        pltpu.make_async_copy(a, b, wsem.at[i])
        for i, (a, b) in enumerate(((wg_ref, wg), (wu_ref, wu), (wd_ref, wd)))
    ]
    for load in loads:
        load.start()

    peers = [at(dx=i) for i in range(1, nx)]
    peers += [at(dy=i) for i in range(1, ny)]
    peers += [at(flip=True), at(dz=1), at(dz=-1)]
    far_steps = (-(half + 1), half, 2 * half, -(2 * half + 1), nt)
    for step in far_steps:
        peers += [at(dz=step)]
        if step != nt:
            peers += [at(dz=-step)]
    barrier = pltpu.get_barrier_semaphore()
    for peer in peers:
        pl.semaphore_signal(barrier, inc=1, device_id=peer, device_id_type=MESH)
    pl.semaphore_wait(barrier, len(peers))

    xcopies = []
    for i in range(1, nx):
        xcopies.append(
            send(cand_ref.at[lax.rem(x + i, nx)], xr.at[i], xs_s.at[i], xs_r.at[i], at(dx=i))
        )

    flying = {}

    def forward(kind, k, way):
        buf = tb if kind == 0 else ib
        sign = -1 if way == 0 else 1
        src = buf.at[own + sign * (k - 1)]
        if kind == 0 and k == 1:
            src = text_ref
        index = (kind * 2 + way) * right_hops + k - 1
        flying[kind, k, way] = send(
            src, buf.at[own + sign * k], hop_s.at[index], hop_r.at[index],
            at(dz=1 if way == 0 else -1),
        )

    def arrive(k):
        for kind in (0, 1):
            for way in (0, 1):
                last = right_hops if way == 0 else left_hops
                if k <= last:
                    flying[kind, k, way].wait_recv()
                    if k < last:
                        forward(kind, k + 1, way)

    forward(0, 1, 0)
    forward(0, 1, 1)
    for copy in xcopies:
        copy.wait_recv()
    for i in range(nx):
        for rel in range(2):
            piece = cand_ref[x, rel] if i == 0 else xr[i, rel]
            mix[rel, cap * i : cap * i + cap, :] = piece.astype(F32)
    for rel in range(2):
        ib[own, rel] = mix[rel].astype(BF16)
    forward(1, 1, 0)
    forward(1, 1, 1)

    def source_slots(phase):
        if phase == 0:
            return [own - half + j for j in range(2 * half)]
        return [j for j in range(half)] + [own + half + j for j in range(half)]

    def gather_rows(phase):
        slots = source_slots(phase)
        for p in range(half):
            pieces = []
            for s in slots[2 * p : 2 * p + 2]:
                pieces.append((text_ref[...] if s == own else tb[s]).astype(F32))
                pieces.append(ib[s, 0].astype(F32))
                pieces.append(ib[s, 1].astype(F32))
            rows = jnp.concatenate(pieces, axis=0).astype(BF16)
            span = 2 * KINDS * ROWS
            xs[phase, span * p : span * p + span, :] = rows[:, :feat]
            cs[phase, span * p : span * p + span, :] = rows[:, feat:]

    def first_dot(phase, which):
        if which < 2:
            out = jnp.dot(xs[phase], (wg, wu)[which][...], preferred_element_type=F32)
        else:
            out = lax.dot_general(
                cs[phase], wd[...], (((1,), (1,)), ((), ())), preferred_element_type=F32
            )
        for j in range(2 * half):
            block = out[j * KINDS * ROWS : (j + 1) * KINDS * ROWS]
            part[phase, j % 2, j // 2, :, :, which * hid : (which + 1) * hid] = (
                block.reshape(KINDS, ROWS, hid).astype(BF16)
            )

    mates = {}

    def start_mate(phase):
        mates[phase] = send(
            part.at[phase, 1 - c], mate.at[phase], mate_s.at[phase], mate_r.at[phase],
            at(flip=True),
        )

    ysends = {}

    def add_mate(phase):
        mates[phase].wait_recv()
        for i in list(range(1, ny)) + [0]:
            yy = lax.rem(y + i, ny)
            total = part[phase, c, yy].astype(F32) + mate[phase, yy].astype(F32)
            summed[phase, i] = total.astype(BF16)
            if i:
                ysends[phase, i] = send(
                    summed.at[phase, i], parts_in.at[phase, i],
                    y_s.at[phase * ny + i], y_r.at[phase * ny + i], at(dy=i),
                )

    gathers = {}

    def middle(phase):
        for i in range(1, ny):
            ysends[phase, i].wait_recv()
        total = summed[phase, 0].astype(F32)
        for i in range(1, ny):
            total = total + parts_in[phase, i].astype(F32)
        gate, up, back = (total[:, :, i * hid : (i + 1) * hid] for i in range(3))
        s = jax.nn.sigmoid(gate)
        dgate = back * up * s * (1.0 + gate * (1.0 - s))
        dup = back * gate * s
        grads[phase, c, y, :, :, :hid] = dgate.astype(BF16)
        grads[phase, c, y, :, :, hid:] = dup.astype(BF16)
        mine = grads.at[phase, c, y]
        for i in range(1, ny):
            gathers[phase, i] = send(
                mine, mine, ag_s.at[phase * ny + i], ag_r.at[phase * ny + i], at(dy=i)
            )
        gathers[phase, 0] = send(
            mine, mine, fw_s.at[phase * ny], fw_r.at[phase * ny], at(flip=True)
        )

    def pass_on(phase):
        for i in range(1, ny):
            gathers[phase, i].wait_recv()
            theirs = grads.at[phase, c, lax.rem(y - i + ny, ny)]
            gathers[phase, -i] = send(
                theirs, theirs, fw_s.at[phase * ny + i], fw_r.at[phase * ny + i], at(flip=True)
            )

    def second_dots(phase):
        for i in range(ny):
            gathers[phase, -i].wait_recv()
        for p in range(half):
            pieces = []
            for j in (2 * p, 2 * p + 1):
                block = grads[phase, j % 2, j // 2].astype(F32)
                pieces.append(block.reshape(KINDS * ROWS, 2 * hid))
            span = 2 * KINDS * ROWS
            ds[phase, span * p : span * p + span, :] = jnp.concatenate(pieces, axis=0).astype(BF16)
        nt_dims = (((1,), (1,)), ((), ()))
        out = lax.dot_general(ds[phase][:, :hid], wg[...], nt_dims, preferred_element_type=F32)
        out = out + lax.dot_general(
            ds[phase][:, hid:], wu[...], nt_dims, preferred_element_type=F32
        )
        for j in range(2 * half):
            block = out[j * KINDS * ROWS : (j + 1) * KINDS * ROWS]
            terms[phase, j] = block.reshape(KINDS, ROWS, feat).astype(BF16)

    chain = {}

    def chain_a(s):
        if s == 1:
            left, right = terms.at[0, 0], terms.at[0, 2 * half - 1]
        else:
            chain["l", s - 1].wait_recv()
            sa_l[s - 2] = (terms[0, s - 1].astype(F32) + ra_l[s - 2].astype(F32)).astype(BF16)
            left = sa_l.at[s - 2]
            if s <= half - 1:
                chain["r", s - 1].wait_recv()
                sa_r[s - 2] = (
                    terms[0, 2 * half - s].astype(F32) + ra_r[s - 2].astype(F32)
                ).astype(BF16)
                right = sa_r.at[s - 2]
        chain["l", s] = send(left, ra_l.at[s - 1], a_s.at[s - 1], a_r.at[s - 1], at(dz=-1))
        if s <= half - 1:
            n = half + s - 1
            chain["r", s] = send(right, ra_r.at[s - 1], a_s.at[n], a_r.at[n], at(dz=1))

    def finish_a():
        chain["l", half].wait_recv()
        total = terms[0, half].astype(F32) + ra_l[half - 1].astype(F32)
        if half > 1:
            chain["r", half - 1].wait_recv()
            total = total + ra_r[half - 2].astype(F32)
        far_a[...] = total[2].astype(BF16)
        chain["f"] = send(far_a, far_a_in, f_s.at[0], f_r.at[0], at(dz=nt))
        return total[:2]

    def chain_b(s):
        moves = (
            ("nl", rn_l, sn_l, s - 1, slice(0, 2), -1, -(half + 1)),
            ("nr", rn_r, sn_r, 2 * half - s, slice(0, 2), 1, half),
            ("fr", rf_r, sf_r, half - s, slice(2, 3), 1, 2 * half),
            ("fl", rf_l, sf_l, half + s - 1, slice(2, 3), -1, -(2 * half + 1)),
        )
        for i, (name, got, made, j, kinds, step, last) in enumerate(moves):
            if s == 1:
                src = terms.at[1, j, kinds]
            else:
                chain[name, s - 1].wait_recv()
                made[s - 2] = (terms[1, j, kinds].astype(F32) + got[s - 2].astype(F32)).astype(BF16)
                src = made.at[s - 2]
            n = i * half + s - 1
            chain[name, s] = send(
                src, got.at[s - 1], b_s.at[n], b_r.at[n], at(dz=last if s == half else step)
            )

    for k in range(1, half + 1):
        arrive(k)
    gather_rows(0)
    loads[0].wait()
    first_dot(0, 0)
    arrive(half + 1)
    loads[1].wait()
    first_dot(0, 1)
    loads[2].wait()
    first_dot(0, 2)
    start_mate(0)
    for k in range(half + 2, right_hops + 1):
        arrive(k)
        if k == half + 2:
            add_mate(0)
    middle(0)
    gather_rows(1)
    first_dot(1, 0)
    first_dot(1, 1)
    pass_on(0)
    first_dot(1, 2)
    start_mate(1)
    second_dots(0)
    chain_a(1)
    add_mate(1)
    for s in range(2, half):
        chain_a(s)
    middle(1)
    if half > 1:
        chain_a(half)
    pass_on(1)
    near = finish_a()
    mix[0, :, :feat] = near[0]
    mix[1, :, :feat] = near[1]
    second_dots(1)
    for s in range(1, half + 1):
        chain_b(s)
    chain["nl", half].wait_recv()
    chain["nr", half].wait_recv()
    last = rn_l[half - 1].astype(F32) + rn_r[half - 1].astype(F32)
    text = (mix[0, :, :feat] + last[0]).astype(BF16).astype(F32)
    close = (mix[1, :, :feat] + last[1]).astype(BF16).astype(F32)
    txt_ref[...] = jnp.where(live_ref[...] > 0, text, 0.0).astype(BF16)
    chain["f"].wait_recv()
    chain["fr", half].wait_recv()
    chain["fl", half].wait_recv()
    distant = (
        far_a_in[...].astype(F32)
        + rf_r[half - 1, 0].astype(F32)
        + rf_l[half - 1, 0].astype(F32)
    ).astype(BF16).astype(F32)
    chosen = jnp.zeros_like(distant)
    column = col_ref[...]
    for i in range(ROWS):
        chosen = jnp.where(column == i, close[i : i + 1, :], chosen)
        chosen = jnp.where(column == ROWS + i, distant[i : i + 1, :], chosen)
    img_ref[...] = chosen.astype(BF16)
    for copy in started:
        copy.wait_send()


def per_device(
    image_slots, image_cot, text_rows, text_cot, destination, text_count, w_gate, w_up, w_down
):
    groups = lax.axis_size("group")
    nt, ndp = lax.axis_size("tp"), lax.axis_size("dp")
    nx, ny = groups // 2, ndp // 2
    slot_dev, feat = image_slots.shape
    hid = w_gate.shape[1]
    cap = slot_dev // groups
    rows = destination.shape[0]
    g = lax.axis_index("group")
    x, upper = g // 2, g % 2
    target = destination[:, 0]
    position = lax.broadcasted_iota(jnp.int32, (rows, rows), 0)
    other = lax.broadcasted_iota(jnp.int32, (rows, rows), 1)
    same = (target[:, None] == target[None, :]) & (other < position)
    rank = jnp.sum(same.astype(jnp.int32), axis=1)
    away = (target % 2 != upper).astype(jnp.int32)
    column = away * ROWS + (x - target // 2 + nx) % nx * cap + rank
    column = jnp.broadcast_to(column[:, None], (rows, feat))
    live = lax.broadcasted_iota(jnp.int32, (rows, feat), 0) < text_count[0]
    both = jnp.concatenate([image_slots, image_cot], axis=1).reshape(nx, 2, cap, 2 * feat)
    both = jnp.where(upper == 0, both, both[:, ::-1])
    text_both = jnp.concatenate([text_rows, text_cot], axis=1)
    half = nt // 4
    span = 2 * half * KINDS * ROWS
    vm, dma = pltpu.VMEM, pltpu.SemaphoreType.DMA
    block = (KINDS, ROWS, feat)
    hops = nt // 2
    scratch = [
        vm((feat, hid), BF16), vm((feat, hid), BF16), vm((hid, feat), BF16),
        vm((nx, 2, cap, 2 * feat), BF16), vm((2, ROWS, 2 * feat), F32),
        vm((nt, ROWS, 2 * feat), BF16), vm((nt, 2, ROWS, 2 * feat), BF16),
        vm((2, span, feat), BF16), vm((2, span, feat), BF16),
        vm((2, 2, ny, KINDS, ROWS, 3 * hid), BF16), vm((2, ny, KINDS, ROWS, 3 * hid), BF16),
        vm((2, ny, KINDS, ROWS, 3 * hid), BF16), vm((2, ny, KINDS, ROWS, 3 * hid), BF16),
        vm((2, 2, ny, KINDS, ROWS, 2 * hid), BF16), vm((2, span, 2 * hid), BF16),
        vm((2, 2 * half, *block), BF16),
        vm((half, *block), BF16), vm((half, *block), BF16),
        vm((half, *block), BF16), vm((half, *block), BF16),
        vm((ROWS, feat), BF16), vm((ROWS, feat), BF16),
        *[vm((half, 2, ROWS, feat), BF16) for _ in range(4)],
        *[vm((half, 1, ROWS, feat), BF16) for _ in range(4)],
        dma((3,)), dma((nx,)), dma((nx,)), dma((4 * hops,)), dma((4 * hops,)),
        dma((2,)), dma((2,)), dma((2 * ny,)), dma((2 * ny,)), dma((2 * ny,)), dma((2 * ny,)),
        dma((2 * ny,)), dma((2 * ny,)), dma((2 * half,)), dma((2 * half,)),
        dma((4 * half,)), dma((4 * half,)), dma((1,)), dma((1,)),
    ]
    whole = pl.BlockSpec(memory_space=pltpu.VMEM)
    apart = pl.BlockSpec(memory_space=pl.ANY)
    out = jax.ShapeDtypeStruct((ROWS, feat), BF16)
    return pl.pallas_call(
        functools.partial(kernel, nx, nt, ny, cap, feat, hid),
        out_shape=(out, out),
        in_specs=[whole] * 4 + [apart] * 3,
        out_specs=(whole, whole),
        scratch_shapes=scratch,
        compiler_params=pltpu.CompilerParams(
            collective_id=0, has_side_effects=True, vmem_limit_bytes=48 << 20
        ),
    )(both, text_both, column, live.astype(jnp.int32), w_gate, w_up, w_down)


def solution(mesh):
    placed = (
        P(("group", "tp"), "dp"),
        P(("group", "tp"), "dp"),
        P(("group", "tp"), "dp"),
        P(("group", "tp"), "dp"),
        P(("group", "tp"), None),
        P(("group", "tp")),
        P("dp", "tp"),
        P("dp", "tp"),
        P("tp", "dp"),
    )
    return jax.shard_map(
        per_device,
        mesh=mesh,
        in_specs=placed,
        out_specs=(P(("group", "tp"), "dp"), P(("group", "tp"), "dp")),
        check_vma=False,
    )
```

```python
import functools

import jax
import jax.numpy as jnp
from jax import lax
from jax.experimental import pallas as pl
from jax.experimental.pallas import tpu as pltpu
from jax.sharding import PartitionSpec as P

MESH = pl.DeviceIdType.MESH
F32 = jnp.float32
BF16 = jnp.bfloat16
ROWS = 8
KINDS = 3
VMEM_BYTES = 67043328


def kernel(
    nx, nt, ny, cap, feat, hid,
    slot_ref, cot_ref, text_ref, tcot_ref, dest_ref, count_ref, wg_ref, wu_ref, wd_ref,
    img_ref, txt_ref,
    wg, wu, wd, cand, xr, mix, rb, xs, cs, part, mate, summed, parts_in, grads, ds, terms,
    ra_l, ra_r, sa_l, sa_r, far_a, far_a_in, got, made, held,
    wsem, xs_s, xs_r, hop_s, hop_r, mate_s, mate_r, y_s, y_r, ag_s, ag_r, fw_s, fw_r,
    a_s, a_r, b_s, b_r, f_s, f_r,
):
    ring = 2 * nt
    right_hops, left_hops = nt // 2, nt // 2 - 1
    half = nt // 4
    own = right_hops
    g, t, d = lax.axis_index("group"), lax.axis_index("tp"), lax.axis_index("dp")
    x, upper, y, c = g // 2, g % 2, d // 2, d % 2
    z = upper * nt + t

    def at(dx=0, dz=0, dy=0, flip=False):
        zz = lax.rem(z + dz + ring, ring)
        xx = lax.rem(x + dx, nx)
        yy = lax.rem(y + dy, ny)
        cc = 1 - c if flip else c
        return {"group": xx * 2 + zz // nt, "tp": lax.rem(zz, nt), "dp": yy * 2 + cc}

    started, arrived = [], []

    def send(src, dst, s, r, device):
        copy = pltpu.make_async_remote_copy(
            src, dst, s, r, device_id=device, device_id_type=MESH
        )
        copy.start()
        started.append(copy)
        return copy

    def landed(copy):
        copy.wait_recv()
        arrived.append(copy)

    loads = [
        pltpu.make_async_copy(a, b, wsem.at[i])
        for i, (a, b) in enumerate(((wg_ref, wg), (wu_ref, wu), (wd_ref, wd)))
    ]
    for load in loads:
        load.start()

    peers = [at(dx=i) for i in range(1, nx)]
    peers += [at(dy=i) for i in range(1, ny)]
    peers += [at(flip=True), at(dz=1), at(dz=-1)]
    barrier = pltpu.get_barrier_semaphore()
    for peer in peers:
        pl.semaphore_signal(barrier, inc=1, device_id=peer, device_id_type=MESH)
    for p, ref in enumerate((slot_ref, cot_ref)):
        rows = ref[...].astype(F32)
        for i in range(2 * nx):
            rel = lax.rem(i % 2 + upper, 2)
            cand[i // 2, rel, p] = rows[i * cap : i * cap + cap].astype(BF16)
    pl.semaphore_wait(barrier, len(peers))

    xcopies = []
    for i in range(1, nx):
        xcopies.append(
            send(cand.at[lax.rem(x + i, nx)], xr.at[i], xs_s.at[i], xs_r.at[i], at(dx=i))
        )

    flying = {}

    def forward(kind, p, k, way):
        sign = -1 if way == 0 else 1
        src = rb.at[own + sign * (k - 1), kind, p]
        if kind == 0 and k == 1:
            src = (text_ref, tcot_ref)[p]
        index = ((kind * 2 + p) * 2 + way) * right_hops + k - 1
        flying[kind, p, k, way] = send(
            src, rb.at[own + sign * k, kind, p], hop_s.at[index], hop_r.at[index],
            at(dz=1 if way == 0 else -1),
        )

    def arrive(k):
        for kind in range(KINDS):
            for p in range(2):
                for way in range(2):
                    last = right_hops if way == 0 else left_hops
                    if k <= last:
                        landed(flying[kind, p, k, way])
                        if k < last:
                            forward(kind, p, k + 1, way)

    for p in range(2):
        forward(0, p, 1, 0)
        forward(0, p, 1, 1)
    for copy in xcopies:
        landed(copy)
    for rel in range(2):
        for p in range(2):
            for i in range(nx):
                piece = cand[x, rel, p] if i == 0 else xr[i, rel, p]
                mix[rel, p, cap * i : cap * i + cap, :] = piece.astype(F32)
            rb[own, 1 + rel, p] = mix[rel, p].astype(BF16)
            forward(1 + rel, p, 1, 0)
            forward(1 + rel, p, 1, 1)

    def source_slots(phase):
        if phase == 0:
            return [own - half + j for j in range(2 * half)]
        return [j for j in range(half)] + [own + half + j for j in range(half)]

    def gather_rows(phase):
        slots = source_slots(phase)
        span = 2 * KINDS * ROWS
        for p, (out, first) in enumerate(((xs, text_ref), (cs, tcot_ref))):
            for q in range(half):
                pieces = []
                for s in slots[2 * q : 2 * q + 2]:
                    for kind in range(KINDS):
                        mine = s == own and kind == 0
                        pieces.append((first[...] if mine else rb[s, kind, p]).astype(F32))
                out[phase, span * q : span * q + span, :] = (
                    jnp.concatenate(pieces, axis=0).astype(BF16)
                )

    mates, ysends, gathers = {}, {}, {}

    def first_dot(phase, which):
        if which < 2:
            out = jnp.dot(xs[phase], (wg, wu)[which][...], preferred_element_type=F32)
        else:
            out = lax.dot_general(
                cs[phase], wd[...], (((1,), (1,)), ((), ())), preferred_element_type=F32
            )
        for j in range(2 * half):
            block = out[j * KINDS * ROWS : (j + 1) * KINDS * ROWS]
            part[phase, which, j % 2, j // 2] = block.reshape(KINDS, ROWS, hid).astype(BF16)
        n = phase * 3 + which
        mates[phase, which] = send(
            part.at[phase, which, 1 - c], mate.at[phase, which], mate_s.at[n], mate_r.at[n],
            at(flip=True),
        )

    def add_mate(phase, which):
        landed(mates[phase, which])
        for i in list(range(1, ny)) + [0]:
            yy = lax.rem(y + i, ny)
            total = part[phase, which, c, yy].astype(F32) + mate[phase, which, yy].astype(F32)
            summed[phase, which, i] = total.astype(BF16)
            if i:
                n = (phase * 3 + which) * ny + i
                ysends[phase, which, i] = send(
                    summed.at[phase, which, i], parts_in.at[phase, which, i],
                    y_s.at[n], y_r.at[n], at(dy=i),
                )

    def total_of(phase, which):
        total = summed[phase, which, 0].astype(F32)
        for i in range(1, ny):
            landed(ysends[phase, which, i])
            total = total + parts_in[phase, which, i].astype(F32)
        return total

    def middle(phase):
        gate = total_of(phase, 0)
        s = jax.nn.sigmoid(gate)
        slope = s * (1.0 + gate * (1.0 - s))
        up = total_of(phase, 1)
        back = total_of(phase, 2)
        grads[phase, c, y, :, :, :hid] = (back * up * slope).astype(BF16)
        grads[phase, c, y, :, :, hid:] = (back * gate * s).astype(BF16)
        mine = grads.at[phase, c, y]
        for i in range(1, ny):
            gathers[phase, i] = send(
                mine, mine, ag_s.at[phase * ny + i], ag_r.at[phase * ny + i], at(dy=i)
            )
        gathers[phase, 0] = send(
            mine, mine, fw_s.at[phase * ny], fw_r.at[phase * ny], at(flip=True)
        )

    def pass_on(phase):
        for i in range(1, ny):
            landed(gathers[phase, i])
            theirs = grads.at[phase, c, lax.rem(y - i + ny, ny)]
            gathers[phase, -i] = send(
                theirs, theirs, fw_s.at[phase * ny + i], fw_r.at[phase * ny + i], at(flip=True)
            )

    def second_dots(phase):
        for i in range(ny):
            landed(gathers[phase, -i])
        span = 2 * KINDS * ROWS
        for q in range(half):
            pieces = []
            for j in (2 * q, 2 * q + 1):
                block = grads[phase, j % 2, j // 2].astype(F32)
                pieces.append(block.reshape(KINDS * ROWS, 2 * hid))
            ds[phase, span * q : span * q + span, :] = jnp.concatenate(pieces, axis=0).astype(BF16)
        dims = (((1,), (1,)), ((), ()))
        out = lax.dot_general(ds[phase][:, :hid], wg[...], dims, preferred_element_type=F32)
        out = out + lax.dot_general(
            ds[phase][:, hid:], wu[...], dims, preferred_element_type=F32
        )
        for j in range(2 * half):
            block = out[j * KINDS * ROWS : (j + 1) * KINDS * ROWS]
            terms[phase, j] = block.reshape(KINDS, ROWS, feat).astype(BF16)

    chain = {}

    def chain_a(s):
        if s == 1:
            left, right = terms.at[0, 0], terms.at[0, 2 * half - 1]
        else:
            landed(chain["l", s - 1])
            sa_l[s - 2] = (terms[0, s - 1].astype(F32) + ra_l[s - 2].astype(F32)).astype(BF16)
            left = sa_l.at[s - 2]
            if s <= half - 1:
                landed(chain["r", s - 1])
                sa_r[s - 2] = (
                    terms[0, 2 * half - s].astype(F32) + ra_r[s - 2].astype(F32)
                ).astype(BF16)
                right = sa_r.at[s - 2]
        chain["l", s] = send(left, ra_l.at[s - 1], a_s.at[s - 1], a_r.at[s - 1], at(dz=-1))
        if s <= half - 1:
            n = half + s - 1
            chain["r", s] = send(right, ra_r.at[s - 1], a_s.at[n], a_r.at[n], at(dz=1))

    def finish_a():
        landed(chain["l", half])
        landed(chain["r", half - 1])
        total = terms[0, half].astype(F32) + ra_l[half - 1].astype(F32)
        total = total + ra_r[half - 2].astype(F32)
        far_a[...] = total[2].astype(BF16)
        chain["f"] = send(far_a, far_a_in, f_s.at[0], f_r.at[0], at(dz=2 * half))
        held[...] = total[:2]

    def chain_b(s):
        moves = (
            (2, half - s, 1, 2 * half),
            (2, half + s - 1, -1, -(2 * half + 1)),
            (0, s - 1, -1, -(half + 1)),
            (0, 2 * half - s, 1, half),
            (1, s - 1, -1, -(half + 1)),
            (1, 2 * half - s, 1, half),
        )
        for i, (kind, j, step, last) in enumerate(moves):
            if s == 1:
                src = terms.at[1, j, kind]
            else:
                landed(chain[i, s - 1])
                total = terms[1, j, kind].astype(F32) + got[i, s - 2].astype(F32)
                if s == half and i == 0:
                    landed(chain["f"])
                    total = total + far_a_in[...].astype(F32)
                made[i, s - 2] = total.astype(BF16)
                src = made.at[i, s - 2]
            n = i * half + s - 1
            chain[i, s] = send(
                src, got.at[i, s - 1], b_s.at[n], b_r.at[n], at(dz=last if s == half else step)
            )

    for k in range(1, half + 1):
        arrive(k)
    gather_rows(0)
    loads[0].wait()
    first_dot(0, 0)
    arrive(half + 1)
    loads[1].wait()
    first_dot(0, 1)
    loads[2].wait()
    first_dot(0, 2)
    for k in range(half + 2, right_hops + 1):
        arrive(k)
        if k == half + 2:
            for which in range(3):
                add_mate(0, which)
    middle(0)
    gather_rows(1)
    first_dot(1, 0)
    first_dot(1, 1)
    add_mate(1, 0)
    first_dot(1, 2)
    add_mate(1, 1)
    pass_on(0)
    add_mate(1, 2)
    second_dots(0)
    chain_a(1)
    for s in range(2, half):
        chain_a(s)
    middle(1)
    chain_a(half)
    pass_on(1)
    finish_a()
    second_dots(1)
    for s in range(1, half + 1):
        chain_b(s)
    for i in range(2, 6):
        landed(chain[i, half])
    text = held[0] + got[2, half - 1].astype(F32) + got[3, half - 1].astype(F32)
    live = lax.broadcasted_iota(jnp.int32, text.shape, 0) < count_ref[0]
    txt_ref[...] = jnp.where(live, text, 0.0).astype(BF16)
    mix[0, 0] = held[1] + got[4, half - 1].astype(F32) + got[5, half - 1].astype(F32)
    landed(chain[0, half])
    landed(chain[1, half])
    mix[0, 1] = got[0, half - 1].astype(F32) + got[1, half - 1].astype(F32)
    targets = [dest_ref[i] for i in range(ROWS)]
    for i in range(ROWS):
        rank = jnp.int32(0)
        for j in range(i):
            rank = rank + jnp.where(targets[j] == targets[i], 1, 0)
        column, away = lax.div(targets[i], 2), lax.rem(targets[i], 2)
        away = jnp.where(away == upper, 0, 1)
        row = lax.rem(x - column + nx, nx) * cap + jnp.minimum(rank, cap - 1)
        mix[1, 0, i : i + 1, :] = mix[0, away, pl.ds(row, 1), :]
    img_ref[...] = mix[1, 0].astype(BF16)
    for copy in started:
        copy.wait_send()


def per_device(
    image_slots, image_cot, text_rows, text_cot, destination, text_count, w_gate, w_up, w_down
):
    groups = lax.axis_size("group")
    nt, ndp = lax.axis_size("tp"), lax.axis_size("dp")
    nx, ny = groups // 2, ndp // 2
    slot_dev, feat = image_slots.shape
    hid = w_gate.shape[1]
    cap = slot_dev // groups
    half = nt // 4
    span = 2 * half * KINDS * ROWS
    vm, dma = pltpu.VMEM, pltpu.SemaphoreType.DMA
    block = (KINDS, ROWS, feat)
    rows = (KINDS, ROWS, hid)
    hops = nt // 2
    scratch = [
        vm((feat, hid), BF16), vm((feat, hid), BF16), vm((hid, feat), BF16),
        vm((nx, 2, 2, cap, feat), BF16), vm((nx, 2, 2, cap, feat), BF16),
        vm((2, 2, ROWS, feat), F32), vm((nt, KINDS, 2, ROWS, feat), BF16),
        vm((2, span, feat), BF16), vm((2, span, feat), BF16),
        vm((2, 3, 2, ny, *rows), BF16), vm((2, 3, ny, *rows), BF16),
        vm((2, 3, ny, *rows), BF16), vm((2, 3, ny, *rows), BF16),
        vm((2, 2, ny, KINDS, ROWS, 2 * hid), BF16), vm((2, span, 2 * hid), BF16),
        vm((2, 2 * half, *block), BF16),
        vm((half, *block), BF16), vm((half, *block), BF16),
        vm((half, *block), BF16), vm((half, *block), BF16),
        vm((ROWS, feat), BF16), vm((ROWS, feat), BF16),
        vm((6, half, ROWS, feat), BF16), vm((6, half, ROWS, feat), BF16),
        vm((2, ROWS, feat), F32),
        dma((3,)), dma((nx,)), dma((nx,)), dma((12 * hops,)), dma((12 * hops,)),
        dma((6,)), dma((6,)), dma((6 * ny,)), dma((6 * ny,)), dma((2 * ny,)), dma((2 * ny,)),
        dma((2 * ny,)), dma((2 * ny,)), dma((2 * half,)), dma((2 * half,)),
        dma((6 * half,)), dma((6 * half,)), dma((1,)), dma((1,)),
    ]
    whole = pl.BlockSpec(memory_space=pltpu.VMEM)
    apart = pl.BlockSpec(memory_space=pl.ANY)
    scalars = pl.BlockSpec(memory_space=pltpu.SMEM)
    out = jax.ShapeDtypeStruct((ROWS, feat), BF16)
    return pl.pallas_call(
        functools.partial(kernel, nx, nt, ny, cap, feat, hid),
        out_shape=(out, out),
        in_specs=[whole] * 4 + [scalars] * 2 + [apart] * 3,
        out_specs=(whole, whole),
        scratch_shapes=scratch,
        compiler_params=pltpu.CompilerParams(
            collective_id=0, has_side_effects=True, vmem_limit_bytes=VMEM_BYTES
        ),
    )(image_slots, image_cot, text_rows, text_cot, destination[:, 0], text_count,
      w_gate, w_up, w_down)


def solution(mesh):
    placed = (
        P(("group", "tp"), "dp"),
        P(("group", "tp"), "dp"),
        P(("group", "tp"), "dp"),
        P(("group", "tp"), "dp"),
        P(("group", "tp"), None),
        P(("group", "tp")),
        P("dp", "tp"),
        P("dp", "tp"),
        P("tp", "dp"),
    )
    return jax.shard_map(
        per_device,
        mesh=mesh,
        in_specs=placed,
        out_specs=(P(("group", "tp"), "dp"), P(("group", "tp"), "dp")),
        check_vma=False,
    )
```

```python
import functools

import jax
import jax.numpy as jnp
from jax import lax
from jax.experimental import pallas as pl
from jax.experimental.pallas import tpu as pltpu
from jax.sharding import PartitionSpec as P

MESH = pl.DeviceIdType.MESH
F32 = jnp.float32
BF16 = jnp.bfloat16
ROWS = 8
KINDS = 3
VMEM_BYTES = 66000000
PART = 4


def kernel(
    nx, nt, ny, cap, feat, hid,
    slot_ref, cot_ref, text_ref, tcot_ref, dest_ref, count_ref, wg_ref, wu_ref, wd_ref,
    img_ref, txt_ref,
    wg, wu, wd, cand, xr, mix, rb, xs, cs, part, mate, summed, parts_in, grads, ds, terms,
    ra_l, ra_r, sa_l, sa_r, got, made, held,
    wsem, xs_s, xs_r, hop_s, hop_r, mate_s, mate_r, y_s, y_r, ag_s, ag_r, fw_s, fw_r,
    a_s, a_r, b_s, b_r,
):
    ring = 2 * nt
    right_hops, left_hops = nt // 2, nt // 2 - 1
    half = nt // 4
    own = right_hops
    g, t, d = lax.axis_index("group"), lax.axis_index("tp"), lax.axis_index("dp")
    x, upper, y, c = g // 2, g % 2, d // 2, d % 2
    z = upper * nt + t

    def at(dx=0, dz=0, dy=0, flip=False):
        zz = lax.rem(z + dz + ring, ring)
        xx = lax.rem(x + dx, nx)
        yy = lax.rem(y + dy, ny)
        cc = 1 - c if flip else c
        return {"group": xx * 2 + zz // nt, "tp": lax.rem(zz, nt), "dp": yy * 2 + cc}

    started, arrived = [], []

    def send(src, dst, s, r, device):
        copy = pltpu.make_async_remote_copy(
            src, dst, s, r, device_id=device, device_id_type=MESH
        )
        copy.start()
        started.append(copy)
        return copy

    def landed(copy):
        copy.wait_recv()
        arrived.append(copy)

    loads = [
        pltpu.make_async_copy(a, b, wsem.at[i])
        for i, (a, b) in enumerate(((wg_ref, wg), (wu_ref, wu), (wd_ref, wd)))
    ]
    for load in loads:
        load.start()

    peers = [at(dx=i) for i in range(1, nx)]
    peers += [at(dy=i) for i in range(1, ny)]
    peers += [at(flip=True), at(dz=1), at(dz=-1)]
    barrier = pltpu.get_barrier_semaphore()
    for peer in peers:
        pl.semaphore_signal(barrier, inc=1, device_id=peer, device_id_type=MESH)
    for p, ref in enumerate((slot_ref, cot_ref)):
        rows = ref[...].astype(F32)
        for i in range(2 * nx):
            rel = lax.rem(i % 2 + upper, 2)
            cand[i // 2, rel, p] = rows[i * cap : i * cap + cap].astype(BF16)
    pl.semaphore_wait(barrier, len(peers))

    xcopies = []
    for i in range(1, nx):
        xcopies.append(
            send(cand.at[lax.rem(x + i, nx)], xr.at[i], xs_s.at[i], xs_r.at[i], at(dx=i))
        )

    flying = {}

    def forward(kind, p, k, way):
        sign = -1 if way == 0 else 1
        src = rb.at[own + sign * (k - 1), kind, p]
        if kind == 0 and k == 1:
            src = (text_ref, tcot_ref)[p]
        index = ((kind * 2 + p) * 2 + way) * right_hops + k - 1
        flying[kind, p, k, way] = send(
            src, rb.at[own + sign * k, kind, p], hop_s.at[index], hop_r.at[index],
            at(dz=1 if way == 0 else -1),
        )

    def arrive(k):
        for kind in range(KINDS):
            for p in range(2):
                for way in range(2):
                    last = right_hops if way == 0 else left_hops
                    if k <= last:
                        landed(flying[kind, p, k, way])
                        if k < last:
                            forward(kind, p, k + 1, way)

    for p in range(2):
        forward(0, p, 1, 0)
        forward(0, p, 1, 1)
    for copy in xcopies:
        landed(copy)
    for rel in range(2):
        for p in range(2):
            for i in range(nx):
                piece = cand[x, rel, p] if i == 0 else xr[i, rel, p]
                mix[rel, p, cap * i : cap * i + cap, :] = piece.astype(F32)
            rb[own, 1 + rel, p] = mix[rel, p].astype(BF16)
            forward(1 + rel, p, 1, 0)
            forward(1 + rel, p, 1, 1)

    def sources(phase):
        inner = [half - 2, half - 1, half, half + 1]
        outer = [0, 1, 2 * half - 2, 2 * half - 1]
        return outer if phase % 2 else inner

    def source_slots(phase):
        if phase < 2:
            return [own - half + j for j in sources(phase)]
        return [j if j < half else own + j for j in sources(phase)]

    def gather_rows(phase):
        slots = source_slots(phase)
        span = 2 * KINDS * ROWS
        for p, (out, first) in enumerate(((xs, text_ref), (cs, tcot_ref))):
            for q in range(half // 2):
                pieces = []
                for s in slots[2 * q : 2 * q + 2]:
                    for kind in range(KINDS):
                        mine = s == own and kind == 0
                        pieces.append((first[...] if mine else rb[s, kind, p]).astype(F32))
                out[phase, span * q : span * q + span, :] = (
                    jnp.concatenate(pieces, axis=0).astype(BF16)
                )

    mates, ysends, gathers = {}, {}, {}

    def first_dot(phase, which):
        if which < 2:
            out = jnp.dot(xs[phase], (wg, wu)[which][...], preferred_element_type=F32)
        else:
            out = lax.dot_general(
                cs[phase], wd[...], (((1,), (1,)), ((), ())), preferred_element_type=F32
            )
        for i in range(ny):
            block = out[i * KINDS * ROWS : (i + 1) * KINDS * ROWS].reshape(KINDS, ROWS, hid)
            for core in range(2):
                part[phase, which, core, i] = block[:, core * PART : core * PART + PART].astype(BF16)
        n = phase * 3 + which
        mates[phase, which] = send(
            part.at[phase, which, 1 - c], mate.at[phase, which], mate_s.at[n], mate_r.at[n],
            at(flip=True),
        )

    def add_mate(phase, which):
        landed(mates[phase, which])
        for i in list(range(1, ny)) + [0]:
            yy = lax.rem(y + i, ny)
            total = part[phase, which, c, yy].astype(F32) + mate[phase, which, yy].astype(F32)
            summed[phase, which, i] = total.astype(BF16)
            if i:
                n = (phase * 3 + which) * ny + i
                ysends[phase, which, i] = send(
                    summed.at[phase, which, i], parts_in.at[phase, which, i],
                    y_s.at[n], y_r.at[n], at(dy=i),
                )

    def total_of(phase, which):
        total = summed[phase, which, 0].astype(F32)
        for i in range(1, ny):
            landed(ysends[phase, which, i])
            total = total + parts_in[phase, which, i].astype(F32)
        return total

    def middle(phase):
        gate = total_of(phase, 0)
        s = jax.nn.sigmoid(gate)
        slope = s * (1.0 + gate * (1.0 - s))
        up = total_of(phase, 1)
        back = total_of(phase, 2)
        grads[phase, c, y, :, :, :hid] = (back * up * slope).astype(BF16)
        grads[phase, c, y, :, :, hid:] = (back * gate * s).astype(BF16)
        mine = grads.at[phase, c, y]
        for i in range(1, ny):
            gathers[phase, i] = send(
                mine, mine, ag_s.at[phase * ny + i], ag_r.at[phase * ny + i], at(dy=i)
            )
        gathers[phase, 0] = send(
            mine, mine, fw_s.at[phase * ny], fw_r.at[phase * ny], at(flip=True)
        )

    def pass_on(phase):
        for i in range(1, ny):
            landed(gathers[phase, i])
            theirs = grads.at[phase, c, lax.rem(y - i + ny, ny)]
            gathers[phase, -i] = send(
                theirs, theirs, fw_s.at[phase * ny + i], fw_r.at[phase * ny + i], at(flip=True)
            )

    def second_dots(phase):
        for i in range(ny):
            landed(gathers[phase, -i])
        span = 2 * KINDS * ROWS
        for q in range(half // 2):
            pieces = []
            for i in (2 * q, 2 * q + 1):
                block = jnp.concatenate(
                    [grads[phase, core, i].astype(F32) for core in range(2)], axis=1
                )
                pieces.append(block.reshape(KINDS * ROWS, 2 * hid))
            ds[phase, span * q : span * q + span, :] = jnp.concatenate(pieces, axis=0).astype(BF16)
        dims = (((1,), (1,)), ((), ()))
        out = lax.dot_general(ds[phase][:, :hid], wg[...], dims, preferred_element_type=F32)
        out = out + lax.dot_general(
            ds[phase][:, hid:], wu[...], dims, preferred_element_type=F32
        )
        for i, j in enumerate(sources(phase)):
            block = out[i * KINDS * ROWS : (i + 1) * KINDS * ROWS]
            terms[phase // 2, j] = block.reshape(KINDS, ROWS, feat).astype(BF16)

    chain = {}
    two = slice(0, 2)

    def chain_a(s):
        if s == 1:
            left, right = terms.at[0, 0, two], terms.at[0, 2 * half - 1, two]
        else:
            landed(chain["l", s - 1])
            sa_l[s - 2] = (terms[0, s - 1, two].astype(F32) + ra_l[s - 2].astype(F32)).astype(BF16)
            left = sa_l.at[s - 2]
            if s <= half - 1:
                landed(chain["r", s - 1])
                sa_r[s - 2] = (
                    terms[0, 2 * half - s, two].astype(F32) + ra_r[s - 2].astype(F32)
                ).astype(BF16)
                right = sa_r.at[s - 2]
        chain["l", s] = send(left, ra_l.at[s - 1], a_s.at[s - 1], a_r.at[s - 1], at(dz=-1))
        if s <= half - 1:
            n = half + s - 1
            chain["r", s] = send(right, ra_r.at[s - 1], a_s.at[n], a_r.at[n], at(dz=1))

    def finish_a():
        landed(chain["l", half])
        landed(chain["r", half - 1])
        total = terms[0, half, two].astype(F32) + ra_l[half - 1].astype(F32)
        held[...] = total + ra_r[half - 2].astype(F32)

    far_r = [(0, half - k, 1) for k in range(half + 1)]
    far_r += [(1, 2 * half - k, 1) for k in range(half + 1, 2 * half)] + [(1, 0, 2 * half)]
    far_l = [(0, half + k, -1) for k in range(1, half)]
    far_l += [(1, k, -1) for k in range(half, 2 * half - 1)] + [(1, 2 * half - 1, -(2 * half + 1))]
    inner_l = [(1, half - 2, -1), (1, half - 1, -(half + 1))]
    inner_r = [(1, half + 1, 1), (1, half, half)]
    outer_l = [(1, 0, -1), (1, 1, -(2 * half - 1))]
    outer_r = [(1, 2 * half - 1, 1), (1, 2 * half - 2, 2 * half - 2)]
    routes = [(2, far_r), (2, far_l)]
    routes += [(kind, way) for way in (inner_l, inner_r, outer_l, outer_r) for kind in (0, 1)]
    first = [sum(len(r[1]) for r in routes[:i]) for i in range(len(routes))]

    def hop_on(i, s):
        kind, steps = routes[i]
        ab, j, dz = steps[s - 1]
        n = first[i] + s - 1
        if s == 1:
            src = terms.at[ab, j, kind]
        else:
            landed(chain[i, s - 1])
            made[n] = (terms[ab, j, kind].astype(F32) + got[n - 1].astype(F32)).astype(BF16)
            src = made.at[n]
        chain[i, s] = send(src, got.at[n], b_s.at[n], b_r.at[n], at(dz=dz))

    def ended(i):
        landed(chain[i, len(routes[i][1])])
        return got[first[i] + len(routes[i][1]) - 1].astype(F32)

    def dots(phase):
        gather_rows(phase)
        for which in range(3):
            if phase == 0:
                loads[which].wait()
            first_dot(phase, which)

    def add_mates(phase):
        for which in range(3):
            add_mate(phase, which)

    arrive(1)
    arrive(2)
    dots(0)
    arrive(3)
    add_mates(0)
    arrive(4)
    dots(1)
    arrive(5)
    add_mates(1)
    middle(0)
    arrive(6)
    dots(2)
    pass_on(0)
    arrive(7)
    add_mates(2)
    middle(1)
    second_dots(0)
    hop_on(0, 1)
    hop_on(1, 1)
    arrive(8)
    gather_rows(3)
    first_dot(3, 0)
    first_dot(3, 1)
    hop_on(0, 2)
    add_mate(3, 0)
    first_dot(3, 2)
    add_mate(3, 1)
    pass_on(1)
    add_mate(3, 2)
    middle(2)
    hop_on(0, 3)
    second_dots(1)
    chain_a(1)
    hop_on(0, 4)
    hop_on(1, 2)
    pass_on(2)
    chain_a(2)
    middle(3)
    hop_on(0, 5)
    hop_on(1, 3)
    second_dots(2)
    for i in range(2, 6):
        hop_on(i, 1)
    hop_on(0, 6)
    hop_on(1, 4)
    chain_a(3)
    pass_on(3)
    hop_on(0, 7)
    hop_on(1, 5)
    second_dots(3)
    for i in range(6, 10):
        hop_on(i, 1)
    hop_on(0, 8)
    hop_on(1, 6)
    chain_a(4)
    for i in range(2, 6):
        hop_on(i, 2)
    hop_on(0, 9)
    hop_on(1, 7)
    for i in range(6, 10):
        hop_on(i, 2)
    finish_a()
    sums = [held[0], held[1]]
    for i in range(2, 10):
        sums[i % 2] = sums[i % 2] + ended(i)
    live = lax.broadcasted_iota(jnp.int32, sums[0].shape, 0) < count_ref[0]
    txt_ref[...] = jnp.where(live, sums[0], 0.0).astype(BF16)
    mix[0, 0] = sums[1]
    mix[0, 1] = ended(0) + ended(1)
    targets = [dest_ref[i] for i in range(ROWS)]
    for i in range(ROWS):
        rank = jnp.int32(0)
        for j in range(i):
            rank = rank + jnp.where(targets[j] == targets[i], 1, 0)
        column, away = lax.div(targets[i], 2), lax.rem(targets[i], 2)
        away = jnp.where(away == upper, 0, 1)
        row = lax.rem(x - column + nx, nx) * cap + jnp.minimum(rank, cap - 1)
        mix[1, 0, i : i + 1, :] = mix[0, away, pl.ds(row, 1), :]
    img_ref[...] = mix[1, 0].astype(BF16)
    for copy in started:
        copy.wait_send()


def per_device(
    image_slots, image_cot, text_rows, text_cot, destination, text_count, w_gate, w_up, w_down
):
    groups = lax.axis_size("group")
    nt, ndp = lax.axis_size("tp"), lax.axis_size("dp")
    nx, ny = groups // 2, ndp // 2
    slot_dev, feat = image_slots.shape
    hid = w_gate.shape[1]
    cap = slot_dev // groups
    half = nt // 4
    vm, dma = pltpu.VMEM, pltpu.SemaphoreType.DMA
    block = (KINDS, ROWS, feat)
    rows = (KINDS, PART, hid)
    hops = nt // 2
    span = half * KINDS * ROWS
    pair = (half, 2, ROWS, feat)
    scratch = [
        vm((feat, hid), BF16), vm((feat, hid), BF16), vm((hid, feat), BF16),
        vm((nx, 2, 2, cap, feat), BF16), vm((nx, 2, 2, cap, feat), BF16),
        vm((2, 2, ROWS, feat), F32), vm((nt, KINDS, 2, ROWS, feat), BF16),
        vm((4, span, feat), BF16), vm((4, span, feat), BF16),
        vm((4, 3, 2, ny, *rows), BF16), vm((4, 3, ny, *rows), BF16),
        vm((4, 3, ny, *rows), BF16), vm((4, 3, ny, *rows), BF16),
        vm((4, 2, ny, KINDS, PART, 2 * hid), BF16), vm((4, span, 2 * hid), BF16),
        vm((2, 2 * half, *block), BF16),
        vm(pair, BF16), vm(pair, BF16), vm(pair, BF16), vm(pair, BF16),
        vm((32, ROWS, feat), BF16), vm((32, ROWS, feat), BF16),
        vm((2, ROWS, feat), F32),
        dma((3,)), dma((nx,)), dma((nx,)), dma((12 * hops,)), dma((12 * hops,)),
        dma((12,)), dma((12,)), dma((12 * ny,)), dma((12 * ny,)), dma((4 * ny,)), dma((4 * ny,)),
        dma((4 * ny,)), dma((4 * ny,)), dma((2 * half,)), dma((2 * half,)),
        dma((32,)), dma((32,)),
    ]
    whole = pl.BlockSpec(memory_space=pltpu.VMEM)
    apart = pl.BlockSpec(memory_space=pl.ANY)
    scalars = pl.BlockSpec(memory_space=pltpu.SMEM)
    out = jax.ShapeDtypeStruct((ROWS, feat), BF16)
    return pl.pallas_call(
        functools.partial(kernel, nx, nt, ny, cap, feat, hid),
        out_shape=(out, out),
        in_specs=[whole] * 4 + [scalars] * 2 + [apart] * 3,
        out_specs=(whole, whole),
        scratch_shapes=scratch,
        compiler_params=pltpu.CompilerParams(
            collective_id=0, has_side_effects=True, vmem_limit_bytes=VMEM_BYTES
        ),
    )(image_slots, image_cot, text_rows, text_cot, destination[:, 0], text_count,
      w_gate, w_up, w_down)


def solution(mesh):
    placed = (
        P(("group", "tp"), "dp"),
        P(("group", "tp"), "dp"),
        P(("group", "tp"), "dp"),
        P(("group", "tp"), "dp"),
        P(("group", "tp"), None),
        P(("group", "tp")),
        P("dp", "tp"),
        P("dp", "tp"),
        P("tp", "dp"),
    )
    return jax.shard_map(
        per_device,
        mesh=mesh,
        in_specs=placed,
        out_specs=(P(("group", "tp"), "dp"), P(("group", "tp"), "dp")),
        check_vma=False,
    )
```

```python
import functools

import jax
import jax.numpy as jnp
from jax import lax
from jax.experimental import pallas as pl
from jax.experimental.pallas import tpu as pltpu
from jax.sharding import PartitionSpec as P

MESH = pl.DeviceIdType.MESH
F32 = jnp.float32
BF16 = jnp.bfloat16
ROWS = 8
KINDS = 3
VMEM_BYTES = 66000000
PART = 4


def kernel(
    nx, nt, ny, cap, feat, hid,
    slot_ref, cot_ref, text_ref, tcot_ref, dest_ref, count_ref, wg_ref, wu_ref, wd_ref,
    out_ref,
    wg, wu, wd, cand, xr, mix, rb, xs, cs, part, mate, summed, parts_in, grads, ds, terms,
    ra_l, ra_r, sa_l, sa_r, got, made, held,
    wsem, xs_s, xs_r, hop_s, hop_r, mate_s, mate_r, y_s, y_r, ag_s, ag_r, fw_s, fw_r,
    a_s, a_r, b_s, b_r,
):
    ring = 2 * nt
    right_hops, left_hops = nt // 2, nt // 2 - 1
    half = nt // 4
    own = right_hops
    g, t, d = lax.axis_index("group"), lax.axis_index("tp"), lax.axis_index("dp")
    x, upper, y, c = g // 2, g % 2, d // 2, d % 2
    z = upper * nt + t

    def at(dx=0, dz=0, dy=0, flip=False):
        zz = lax.rem(z + dz + ring, ring)
        xx = lax.rem(x + dx, nx)
        yy = lax.rem(y + dy, ny)
        cc = 1 - c if flip else c
        return {"group": xx * 2 + zz // nt, "tp": lax.rem(zz, nt), "dp": yy * 2 + cc}

    started, arrived = [], []

    def send(src, dst, s, r, device):
        copy = pltpu.make_async_remote_copy(
            src, dst, s, r, device_id=device, device_id_type=MESH
        )
        copy.start()
        started.append(copy)
        return copy

    def landed(copy):
        copy.wait_recv()
        arrived.append(copy)

    loads = [
        pltpu.make_async_copy(a, b, wsem.at[i])
        for i, (a, b) in enumerate(((wg_ref, wg), (wu_ref, wu), (wd_ref, wd)))
    ]
    for load in loads:
        load.start()

    peers = [at(dx=i) for i in range(1, nx)]
    peers += [at(dy=i) for i in range(1, ny)]
    peers += [at(flip=True), at(dz=1), at(dz=-1), at(dz=2), at(dz=-2)]
    barrier = pltpu.get_barrier_semaphore()
    for peer in peers:
        pl.semaphore_signal(barrier, inc=1, device_id=peer, device_id_type=MESH)
    for p, ref in enumerate((slot_ref, cot_ref)):
        rows = ref[...].astype(F32)
        for i in range(2 * nx):
            rel = lax.rem(i % 2 + upper, 2)
            cand[i // 2, rel, p] = rows[i * cap : i * cap + cap].astype(BF16)
    pl.semaphore_wait(barrier, len(peers))

    xcopies = []
    for i in range(1, nx):
        xcopies.append(
            send(cand.at[lax.rem(x + i, nx)], xr.at[i], xs_s.at[i], xs_r.at[i], at(dx=i))
        )

    flying = {}

    def forward(kind, p, k, way):
        sign = -1 if way == 0 else 1
        hops = k if k < 3 else 1
        src = rb.at[own + sign * (k - hops), kind, p]
        if kind == 0 and k < 3:
            src = (text_ref, tcot_ref)[p]
        index = ((kind * 2 + p) * 2 + way) * right_hops + k - 1
        flying[kind, p, k, way] = send(
            src, rb.at[own + sign * k, kind, p], hop_s.at[index], hop_r.at[index],
            at(dz=hops if way == 0 else -hops),
        )

    def begin(kind, p):
        for k in (2, 1):
            forward(kind, p, k, 0)
            forward(kind, p, k, 1)

    def arrive(k):
        for kind in range(KINDS):
            for p in range(2):
                for way in range(2):
                    last = right_hops if way == 0 else left_hops
                    if k <= last:
                        landed(flying[kind, p, k, way])
                        if 1 < k < last:
                            forward(kind, p, k + 1, way)

    for p in range(2):
        begin(0, p)
    for copy in xcopies:
        landed(copy)
    for rel in range(2):
        for p in range(2):
            for i in range(nx):
                piece = cand[x, rel, p] if i == 0 else xr[i, rel, p]
                mix[rel, p, cap * i : cap * i + cap, :] = piece.astype(F32)
            rb[own, 1 + rel, p] = mix[rel, p].astype(BF16)
            begin(1 + rel, p)

    def sources(phase):
        inner = [half - 2, half - 1, half, half + 1]
        outer = [0, 1, 2 * half - 2, 2 * half - 1]
        return outer if phase % 2 else inner

    def source_slots(phase):
        if phase < 2:
            return [own - half + j for j in sources(phase)]
        return [j if j < half else own + j for j in sources(phase)]

    def gather_rows(phase):
        slots = source_slots(phase)
        span = 2 * KINDS * ROWS
        for p, (out, first) in enumerate(((xs, text_ref), (cs, tcot_ref))):
            for q in range(half // 2):
                pieces = []
                for s in slots[2 * q : 2 * q + 2]:
                    for kind in range(KINDS):
                        mine = s == own and kind == 0
                        pieces.append((first[...] if mine else rb[s, kind, p]).astype(F32))
                out[phase, span * q : span * q + span, :] = (
                    jnp.concatenate(pieces, axis=0).astype(BF16)
                )

    mates, ysends, gathers = {}, {}, {}

    def first_dot(phase, which):
        if which < 2:
            out = jnp.dot(xs[phase], (wg, wu)[which][...], preferred_element_type=F32)
        else:
            out = lax.dot_general(
                cs[phase], wd[...], (((1,), (1,)), ((), ())), preferred_element_type=F32
            )
        for i in range(ny):
            block = out[i * KINDS * ROWS : (i + 1) * KINDS * ROWS].reshape(KINDS, ROWS, hid)
            for core in range(2):
                part[phase, which, core, i] = block[:, core * PART : core * PART + PART].astype(BF16)
        n = phase * 3 + which
        mates[phase, which] = send(
            part.at[phase, which, 1 - c], mate.at[phase, which], mate_s.at[n], mate_r.at[n],
            at(flip=True),
        )

    def add_mate(phase, which):
        landed(mates[phase, which])
        for i in list(range(1, ny)) + [0]:
            yy = lax.rem(y + i, ny)
            total = part[phase, which, c, yy].astype(F32) + mate[phase, which, yy].astype(F32)
            summed[phase, which, i] = total.astype(BF16)
            if i:
                n = (phase * 3 + which) * ny + i
                ysends[phase, which, i] = send(
                    summed.at[phase, which, i], parts_in.at[phase, which, i],
                    y_s.at[n], y_r.at[n], at(dy=i),
                )

    def total_of(phase, which):
        total = summed[phase, which, 0].astype(F32)
        for i in range(1, ny):
            landed(ysends[phase, which, i])
            total = total + parts_in[phase, which, i].astype(F32)
        return total

    def middle(phase):
        gate = total_of(phase, 0)
        s = jax.nn.sigmoid(gate)
        slope = s * (1.0 + gate * (1.0 - s))
        up = total_of(phase, 1)
        back = total_of(phase, 2)
        grads[phase, c, y, :, :, :hid] = (back * up * slope).astype(BF16)
        grads[phase, c, y, :, :, hid:] = (back * gate * s).astype(BF16)
        mine = grads.at[phase, c, y]
        for i in range(1, ny):
            gathers[phase, i] = send(
                mine, mine, ag_s.at[phase * ny + i], ag_r.at[phase * ny + i], at(dy=i)
            )
        gathers[phase, 0] = send(
            mine, mine, fw_s.at[phase * ny], fw_r.at[phase * ny], at(flip=True)
        )

    def pass_on(phase):
        for i in range(1, ny):
            landed(gathers[phase, i])
            theirs = grads.at[phase, c, lax.rem(y - i + ny, ny)]
            gathers[phase, -i] = send(
                theirs, theirs, fw_s.at[phase * ny + i], fw_r.at[phase * ny + i], at(flip=True)
            )

    def second_dots(phase):
        for i in range(ny):
            landed(gathers[phase, -i])
        span = 2 * KINDS * ROWS
        for q in range(half // 2):
            pieces = []
            for i in (2 * q, 2 * q + 1):
                block = jnp.concatenate(
                    [grads[phase, core, i].astype(F32) for core in range(2)], axis=1
                )
                pieces.append(block.reshape(KINDS * ROWS, 2 * hid))
            ds[phase, span * q : span * q + span, :] = jnp.concatenate(pieces, axis=0).astype(BF16)
        dims = (((1,), (1,)), ((), ()))
        out = lax.dot_general(ds[phase][:, :hid], wg[...], dims, preferred_element_type=F32)
        out = out + lax.dot_general(
            ds[phase][:, hid:], wu[...], dims, preferred_element_type=F32
        )
        for i, j in enumerate(sources(phase)):
            block = out[i * KINDS * ROWS : (i + 1) * KINDS * ROWS]
            terms[phase // 2, j] = block.reshape(KINDS, ROWS, feat).astype(BF16)

    chain = {}
    two = slice(0, 2)

    def chain_a(s):
        if s == 1:
            left, right = terms.at[0, 0, two], terms.at[0, 2 * half - 1, two]
        else:
            landed(chain["l", s - 1])
            sa_l[s - 2] = (terms[0, s - 1, two].astype(F32) + ra_l[s - 2].astype(F32)).astype(BF16)
            left = sa_l.at[s - 2]
            if s <= half - 1:
                landed(chain["r", s - 1])
                sa_r[s - 2] = (
                    terms[0, 2 * half - s, two].astype(F32) + ra_r[s - 2].astype(F32)
                ).astype(BF16)
                right = sa_r.at[s - 2]
        chain["l", s] = send(left, ra_l.at[s - 1], a_s.at[s - 1], a_r.at[s - 1], at(dz=-1))
        if s <= half - 1:
            n = half + s - 1
            chain["r", s] = send(right, ra_r.at[s - 1], a_s.at[n], a_r.at[n], at(dz=1))

    def finish_a():
        landed(chain["l", half])
        landed(chain["r", half - 1])
        total = terms[0, half, two].astype(F32) + ra_l[half - 1].astype(F32)
        held[...] = total + ra_r[half - 2].astype(F32)

    far_r = [(0, half - k, 1) for k in range(half)] + [(0, 0, half)]
    far_l = [(0, half + k, -1) for k in range(1, half - 1)] + [(0, 2 * half - 1, -half)]
    end_r = [(1, half - k, 1) for k in range(1, half)] + [(1, 0, 2 * half)]
    end_l = [(1, half + k, -1) for k in range(half - 1)] + [(1, 2 * half - 1, -(2 * half + 1))]
    inner_l = [(1, half - 2, -1), (1, half - 1, -(half + 1))]
    inner_r = [(1, half + 1, 1), (1, half, half)]
    outer_l = [(1, 0, -1), (1, 1, -(2 * half - 1))]
    outer_r = [(1, 2 * half - 1, 1), (1, 2 * half - 2, 2 * half - 2)]
    routes = [(2, far_r), (2, far_l)]
    routes += [(kind, way) for way in (inner_l, inner_r, outer_l, outer_r) for kind in (0, 1)]
    routes += [(2, end_r), (2, end_l)]
    first = [sum(len(r[1]) for r in routes[:i]) for i in range(len(routes))]

    def hop_on(i, s):
        kind, steps = routes[i]
        ab, j, dz = steps[s - 1]
        n = first[i] + s - 1
        if s == 1:
            src = terms.at[ab, j, kind]
        else:
            landed(chain[i, s - 1])
            total = terms[ab, j, kind].astype(F32) + got[n - 1].astype(F32)
            if i >= 10 and s == len(steps):
                total = total + ended(i - 10)
            made[n] = total.astype(BF16)
            src = made.at[n]
        chain[i, s] = send(src, got.at[n], b_s.at[n], b_r.at[n], at(dz=dz))

    def ended(i):
        landed(chain[i, len(routes[i][1])])
        return got[first[i] + len(routes[i][1]) - 1].astype(F32)

    def dots(phase):
        gather_rows(phase)
        for which in range(3):
            if phase == 0:
                loads[which].wait()
            first_dot(phase, which)

    def add_mates(phase):
        for which in range(3):
            add_mate(phase, which)

    arrive(1)
    arrive(2)
    dots(0)
    arrive(3)
    add_mates(0)
    arrive(4)
    dots(1)
    arrive(5)
    add_mates(1)
    middle(0)
    arrive(6)
    dots(2)
    pass_on(0)
    arrive(7)
    add_mates(2)
    middle(1)
    second_dots(0)
    hop_on(0, 1)
    hop_on(1, 1)
    arrive(8)
    gather_rows(3)
    first_dot(3, 0)
    first_dot(3, 1)
    add_mate(3, 0)
    first_dot(3, 2)
    add_mate(3, 1)
    hop_on(0, 2)
    pass_on(1)
    add_mate(3, 2)
    middle(2)
    second_dots(1)
    chain_a(1)
    hop_on(0, 3)
    hop_on(1, 2)
    chain_a(2)
    hop_on(0, 4)
    hop_on(1, 3)
    pass_on(2)
    middle(3)
    second_dots(2)
    hop_on(10, 1)
    hop_on(11, 1)
    for i in range(2, 6):
        hop_on(i, 1)
    hop_on(0, 5)
    chain_a(3)
    pass_on(3)
    hop_on(10, 2)
    hop_on(11, 2)
    for i in range(2, 6):
        hop_on(i, 2)
    second_dots(3)
    for i in range(6, 10):
        hop_on(i, 1)
    hop_on(10, 3)
    hop_on(11, 3)
    chain_a(4)
    for i in range(6, 10):
        hop_on(i, 2)
    hop_on(10, 4)
    hop_on(11, 4)
    finish_a()
    sums = [held[0], held[1]]
    for i in range(2, 10):
        sums[i % 2] = sums[i % 2] + ended(i)
    live = lax.broadcasted_iota(jnp.int32, sums[0].shape, 0) < count_ref[0]
    out_ref[1] = jnp.where(live, sums[0], 0.0).astype(BF16)
    mix[0, 0] = sums[1]
    mix[0, 1] = ended(10) + ended(11)
    targets = [dest_ref[i] for i in range(ROWS)]
    for i in range(ROWS):
        rank = jnp.int32(0)
        for j in range(i):
            rank = rank + jnp.where(targets[j] == targets[i], 1, 0)
        column, away = lax.div(targets[i], 2), lax.rem(targets[i], 2)
        away = jnp.where(away == upper, 0, 1)
        row = lax.rem(x - column + nx, nx) * cap + jnp.minimum(rank, cap - 1)
        mix[1, 0, i : i + 1, :] = mix[0, away, pl.ds(row, 1), :]
    out_ref[0] = mix[1, 0].astype(BF16)
    for copy in started:
        copy.wait_send()


def per_device(
    image_slots, image_cot, text_rows, text_cot, destination, text_count, w_gate, w_up, w_down
):
    groups = lax.axis_size("group")
    nt, ndp = lax.axis_size("tp"), lax.axis_size("dp")
    nx, ny = groups // 2, ndp // 2
    slot_dev, feat = image_slots.shape
    hid = w_gate.shape[1]
    cap = slot_dev // groups
    half = nt // 4
    vm, dma = pltpu.VMEM, pltpu.SemaphoreType.DMA
    block = (KINDS, ROWS, feat)
    rows = (KINDS, PART, hid)
    hops = nt // 2
    span = half * KINDS * ROWS
    pair = (half, 2, ROWS, feat)
    scratch = [
        vm((feat, hid), BF16), vm((feat, hid), BF16), vm((hid, feat), BF16),
        vm((nx, 2, 2, cap, feat), BF16), vm((nx, 2, 2, cap, feat), BF16),
        vm((2, 2, ROWS, feat), F32), vm((nt, KINDS, 2, ROWS, feat), BF16),
        vm((4, span, feat), BF16), vm((4, span, feat), BF16),
        vm((4, 3, 2, ny, *rows), BF16), vm((4, 3, ny, *rows), BF16),
        vm((4, 3, ny, *rows), BF16), vm((4, 3, ny, *rows), BF16),
        vm((4, 2, ny, KINDS, PART, 2 * hid), BF16), vm((4, span, 2 * hid), BF16),
        vm((2, 2 * half, *block), BF16),
        vm(pair, BF16), vm(pair, BF16), vm(pair, BF16), vm(pair, BF16),
        vm((32, ROWS, feat), BF16), vm((32, ROWS, feat), BF16),
        vm((2, ROWS, feat), F32),
        dma((3,)), dma((nx,)), dma((nx,)), dma((12 * hops,)), dma((12 * hops,)),
        dma((12,)), dma((12,)), dma((12 * ny,)), dma((12 * ny,)), dma((4 * ny,)), dma((4 * ny,)),
        dma((4 * ny,)), dma((4 * ny,)), dma((2 * half,)), dma((2 * half,)),
        dma((32,)), dma((32,)),
    ]
    whole = pl.BlockSpec(memory_space=pltpu.VMEM)
    apart = pl.BlockSpec(memory_space=pl.ANY)
    scalars = pl.BlockSpec(memory_space=pltpu.SMEM)
    out = jax.ShapeDtypeStruct((2, ROWS, feat), BF16)
    grads = pl.pallas_call(
        functools.partial(kernel, nx, nt, ny, cap, feat, hid),
        out_shape=out,
        in_specs=[whole] * 4 + [scalars] * 2 + [apart] * 3,
        out_specs=whole,
        scratch_shapes=scratch,
        compiler_params=pltpu.CompilerParams(
            collective_id=0, has_side_effects=True, vmem_limit_bytes=VMEM_BYTES
        ),
    )(image_slots, image_cot, text_rows, text_cot, destination[:, 0], text_count,
      w_gate, w_up, w_down)
    return grads[0], grads[1]


def solution(mesh):
    placed = (
        P(("group", "tp"), "dp"),
        P(("group", "tp"), "dp"),
        P(("group", "tp"), "dp"),
        P(("group", "tp"), "dp"),
        P(("group", "tp"), None),
        P(("group", "tp")),
        P("dp", "tp"),
        P("dp", "tp"),
        P("tp", "dp"),
    )
    return jax.shard_map(
        per_device,
        mesh=mesh,
        in_specs=placed,
        out_specs=(P(("group", "tp"), "dp"), P(("group", "tp"), "dp")),
        check_vma=False,
    )
```

```python
import functools

import jax
import jax.numpy as jnp
from jax import lax
from jax.experimental import pallas as pl
from jax.experimental.pallas import tpu as pltpu
from jax.sharding import PartitionSpec as P

MESH = pl.DeviceIdType.MESH
F32 = jnp.float32
BF16 = jnp.bfloat16
ROWS = 8
KINDS = 3
VMEM_BYTES = 66000000
PART = 4


def kernel(
    nx, nt, ny, cap, feat, hid,
    slot_ref, cot_ref, text_ref, tcot_ref, dest_ref, count_ref, wg_ref, wu_ref, wd_ref,
    out_ref,
    wg, wu, wd, cand, xr, mix, rb, xs, cs, part, mate, summed, parts_in, grads, ds, terms,
    ra_l, ra_r, sa_l, sa_r, got, made, held,
    wsem, xs_s, xs_r, hop_s, hop_r, mate_s, mate_r, y_s, y_r, ag_s, ag_r, fw_s, fw_r,
    a_s, a_r, b_s, b_r,
):
    ring = 2 * nt
    right_hops, left_hops = nt // 2, nt // 2 - 1
    half = nt // 4
    own = right_hops
    g, t, d = lax.axis_index("group"), lax.axis_index("tp"), lax.axis_index("dp")
    x, upper, y, c = g // 2, g % 2, d // 2, d % 2
    z = upper * nt + t

    def at(dx=0, dz=0, dy=0, flip=False):
        zz = lax.rem(z + dz + ring, ring)
        xx = lax.rem(x + dx, nx)
        yy = lax.rem(y + dy, ny)
        cc = 1 - c if flip else c
        return {"group": xx * 2 + zz // nt, "tp": lax.rem(zz, nt), "dp": yy * 2 + cc}

    started, arrived = [], []

    def send(src, dst, s, r, device):
        copy = pltpu.make_async_remote_copy(
            src, dst, s, r, device_id=device, device_id_type=MESH
        )
        copy.start()
        started.append(copy)
        return copy

    def landed(copy):
        copy.wait_recv()
        arrived.append(copy)

    loads = [
        pltpu.make_async_copy(a, b, wsem.at[i])
        for i, (a, b) in enumerate(((wg_ref, wg), (wu_ref, wu), (wd_ref, wd)))
    ]
    for load in loads:
        load.start()

    peers = [at(dx=i) for i in range(1, nx)]
    peers += [at(dy=i) for i in range(1, ny)]
    peers += [at(flip=True), at(dz=1), at(dz=-1), at(dz=2), at(dz=-2)]
    barrier = pltpu.get_barrier_semaphore()
    for peer in peers:
        pl.semaphore_signal(barrier, inc=1, device_id=peer, device_id_type=MESH)
    for p, ref in enumerate((slot_ref, cot_ref)):
        rows = ref[...].astype(F32)
        for i in range(2 * nx):
            rel = lax.rem(i % 2 + upper, 2)
            cand[i // 2, rel, p] = rows[i * cap : i * cap + cap].astype(BF16)
    pl.semaphore_wait(barrier, len(peers))

    xcopies = []
    for i in range(1, nx):
        xcopies.append(
            send(cand.at[lax.rem(x + i, nx)], xr.at[i], xs_s.at[i], xs_r.at[i], at(dx=i))
        )

    flying = {}

    def forward(kind, p, k, way):
        sign = -1 if way == 0 else 1
        hops = k if k < 3 else 1
        src = rb.at[own + sign * (k - hops), kind, p]
        if kind == 0 and k < 3:
            src = (text_ref, tcot_ref)[p]
        index = ((kind * 2 + p) * 2 + way) * right_hops + k - 1
        flying[kind, p, k, way] = send(
            src, rb.at[own + sign * k, kind, p], hop_s.at[index], hop_r.at[index],
            at(dz=hops if way == 0 else -hops),
        )

    def begin(kind, p):
        for k in (2, 1):
            forward(kind, p, k, 0)
            forward(kind, p, k, 1)

    def arrive(k):
        for kind in range(KINDS):
            for p in range(2):
                for way in range(2):
                    last = right_hops if way == 0 else left_hops
                    if k <= last:
                        landed(flying[kind, p, k, way])
                        if 1 < k < last:
                            forward(kind, p, k + 1, way)

    for p in range(2):
        begin(0, p)
    for copy in xcopies:
        landed(copy)
    for rel in range(2):
        for p in range(2):
            for i in range(nx):
                piece = cand[x, rel, p] if i == 0 else xr[i, rel, p]
                mix[rel, p, cap * i : cap * i + cap, :] = piece.astype(F32)
            rb[own, 1 + rel, p] = mix[rel, p].astype(BF16)
            begin(1 + rel, p)

    def sources(phase):
        inner = [half - 2, half - 1, half, half + 1]
        outer = [0, 1, 2 * half - 2, 2 * half - 1]
        return outer if phase % 2 else inner

    def source_slots(phase):
        if phase < 2:
            return [own - half + j for j in sources(phase)]
        return [j if j < half else own + j for j in sources(phase)]

    def gather_rows(phase):
        slots = source_slots(phase)
        span = 2 * KINDS * ROWS
        for p, (out, first) in enumerate(((xs, text_ref), (cs, tcot_ref))):
            for q in range(half // 2):
                pieces = []
                for s in slots[2 * q : 2 * q + 2]:
                    for kind in range(KINDS):
                        mine = s == own and kind == 0
                        pieces.append((first[...] if mine else rb[s, kind, p]).astype(F32))
                out[phase, span * q : span * q + span, :] = (
                    jnp.concatenate(pieces, axis=0).astype(BF16)
                )

    mates, ysends, gathers = {}, {}, {}

    def first_dot(phase, which):
        if which < 2:
            out = jnp.dot(xs[phase], (wg, wu)[which][...], preferred_element_type=F32)
        else:
            out = lax.dot_general(
                cs[phase], wd[...], (((1,), (1,)), ((), ())), preferred_element_type=F32
            )
        for i in range(ny):
            block = out[i * KINDS * ROWS : (i + 1) * KINDS * ROWS].reshape(KINDS, ROWS, hid)
            for core in range(2):
                part[phase, which, core, i] = block[:, core * PART : core * PART + PART].astype(BF16)
        n = phase * 3 + which
        mates[phase, which] = send(
            part.at[phase, which, 1 - c], mate.at[phase, which], mate_s.at[n], mate_r.at[n],
            at(flip=True),
        )

    def add_mate(phase, which):
        landed(mates[phase, which])
        for i in list(range(1, ny)) + [0]:
            yy = lax.rem(y + i, ny)
            total = part[phase, which, c, yy].astype(F32) + mate[phase, which, yy].astype(F32)
            summed[phase, which, i] = total.astype(BF16)
            if i:
                n = (phase * 3 + which) * ny + i
                ysends[phase, which, i] = send(
                    summed.at[phase, which, i], parts_in.at[phase, which, i],
                    y_s.at[n], y_r.at[n], at(dy=i),
                )

    def total_of(phase, which):
        total = summed[phase, which, 0].astype(F32)
        for i in range(1, ny):
            landed(ysends[phase, which, i])
            total = total + parts_in[phase, which, i].astype(F32)
        return total

    def middle(phase):
        gate = total_of(phase, 0)
        s = jax.nn.sigmoid(gate)
        slope = s * (1.0 + gate * (1.0 - s))
        up = total_of(phase, 1)
        back = total_of(phase, 2)
        grads[phase, c, y, :, :, :hid] = (back * up * slope).astype(BF16)
        grads[phase, c, y, :, :, hid:] = (back * gate * s).astype(BF16)
        mine = grads.at[phase, c, y]
        for i in range(1, ny):
            gathers[phase, i] = send(
                mine, mine, ag_s.at[phase * ny + i], ag_r.at[phase * ny + i], at(dy=i)
            )
        gathers[phase, 0] = send(
            mine, mine, fw_s.at[phase * ny], fw_r.at[phase * ny], at(flip=True)
        )

    def pass_on(phase):
        for i in range(1, ny):
            landed(gathers[phase, i])
            theirs = grads.at[phase, c, lax.rem(y - i + ny, ny)]
            gathers[phase, -i] = send(
                theirs, theirs, fw_s.at[phase * ny + i], fw_r.at[phase * ny + i], at(flip=True)
            )

    def second_dots(phase):
        for i in range(ny):
            landed(gathers[phase, -i])
        span = 2 * KINDS * ROWS
        for q in range(half // 2):
            pieces = []
            for i in (2 * q, 2 * q + 1):
                block = jnp.concatenate(
                    [grads[phase, core, i].astype(F32) for core in range(2)], axis=1
                )
                pieces.append(block.reshape(KINDS * ROWS, 2 * hid))
            ds[phase, span * q : span * q + span, :] = jnp.concatenate(pieces, axis=0).astype(BF16)
        dims = (((1,), (1,)), ((), ()))
        out = lax.dot_general(ds[phase][:, :hid], wg[...], dims, preferred_element_type=F32)
        out = out + lax.dot_general(
            ds[phase][:, hid:], wu[...], dims, preferred_element_type=F32
        )
        for i, j in enumerate(sources(phase)):
            block = out[i * KINDS * ROWS : (i + 1) * KINDS * ROWS]
            terms[phase // 2, j] = block.reshape(KINDS, ROWS, feat).astype(BF16)

    chain = {}
    two = slice(0, 2)

    def chain_a(s):
        if s == 1:
            left, right = terms.at[0, 0, two], terms.at[0, 2 * half - 1, two]
        else:
            landed(chain["l", s - 1])
            sa_l[s - 2] = (terms[0, s - 1, two].astype(F32) + ra_l[s - 2].astype(F32)).astype(BF16)
            left = sa_l.at[s - 2]
            if s <= half - 1:
                landed(chain["r", s - 1])
                sa_r[s - 2] = (
                    terms[0, 2 * half - s, two].astype(F32) + ra_r[s - 2].astype(F32)
                ).astype(BF16)
                right = sa_r.at[s - 2]
        chain["l", s] = send(left, ra_l.at[s - 1], a_s.at[s - 1], a_r.at[s - 1], at(dz=-1))
        if s <= half - 1:
            n = half + s - 1
            chain["r", s] = send(right, ra_r.at[s - 1], a_s.at[n], a_r.at[n], at(dz=1))

    def finish_a():
        landed(chain["l", half])
        landed(chain["r", half - 1])
        total = terms[0, half, two].astype(F32) + ra_l[half - 1].astype(F32)
        held[...] = total + ra_r[half - 2].astype(F32)

    far_r = [(0, half - k, 1) for k in range(half)] + [(0, 0, half)]
    far_l = [(0, half + k, -1) for k in range(1, half - 1)] + [(0, 2 * half - 1, -half)]
    end_r = [(1, half - k, 1) for k in range(1, half)] + [(1, 0, 2 * half)]
    end_l = [(1, half + k, -1) for k in range(half - 1)] + [(1, 2 * half - 1, -(2 * half + 1))]
    inner_l = [(1, half - 2, -1), (1, half - 1, -(half + 1))]
    inner_r = [(1, half + 1, 1), (1, half, half)]
    outer_l = [(1, 0, -1), (1, 1, -(2 * half - 1))]
    outer_r = [(1, 2 * half - 1, 1), (1, 2 * half - 2, 2 * half - 2)]
    routes = [(2, far_r), (2, far_l)]
    routes += [(kind, way) for way in (inner_l, inner_r, outer_l, outer_r) for kind in (0, 1)]
    routes += [(2, end_r), (2, end_l)]
    first = [sum(len(r[1]) for r in routes[:i]) for i in range(len(routes))]

    def hop_on(i, s):
        kind, steps = routes[i]
        ab, j, dz = steps[s - 1]
        n = first[i] + s - 1
        if s == 1:
            src = terms.at[ab, j, kind]
        else:
            landed(chain[i, s - 1])
            total = terms[ab, j, kind].astype(F32) + got[n - 1].astype(F32)
            if i >= 10 and s == len(steps):
                total = total + ended(i - 10)
            made[n] = total.astype(BF16)
            src = made.at[n]
        chain[i, s] = send(src, got.at[n], b_s.at[n], b_r.at[n], at(dz=dz))

    def ended(i):
        landed(chain[i, len(routes[i][1])])
        return got[first[i] + len(routes[i][1]) - 1].astype(F32)

    def dots(phase):
        gather_rows(phase)
        for which in range(3):
            if phase == 0:
                loads[which].wait()
            first_dot(phase, which)

    def add_mates(phase):
        for which in range(3):
            add_mate(phase, which)

    arrive(1)
    arrive(2)
    dots(0)
    arrive(3)
    add_mates(0)
    arrive(4)
    dots(1)
    arrive(5)
    add_mates(1)
    arrive(6)
    middle(0)
    dots(2)
    arrive(7)
    add_mates(2)
    pass_on(0)
    middle(1)
    arrive(8)
    gather_rows(3)
    first_dot(3, 0)
    first_dot(3, 1)
    add_mate(3, 0)
    first_dot(3, 2)
    add_mate(3, 1)
    second_dots(0)
    hop_on(0, 1)
    hop_on(1, 1)
    add_mate(3, 2)
    pass_on(1)
    middle(2)
    second_dots(1)
    chain_a(1)
    hop_on(0, 2)
    hop_on(1, 2)
    chain_a(2)
    pass_on(2)
    middle(3)
    hop_on(0, 3)
    hop_on(1, 3)
    second_dots(2)
    hop_on(10, 1)
    hop_on(11, 1)
    for i in range(2, 6):
        hop_on(i, 1)
    hop_on(0, 4)
    chain_a(3)
    pass_on(3)
    hop_on(10, 2)
    hop_on(11, 2)
    for i in range(2, 6):
        hop_on(i, 2)
    hop_on(0, 5)
    second_dots(3)
    for i in range(6, 10):
        hop_on(i, 1)
    hop_on(10, 3)
    hop_on(11, 3)
    chain_a(4)
    for i in range(6, 10):
        hop_on(i, 2)
    hop_on(10, 4)
    hop_on(11, 4)
    finish_a()
    sums = [held[0], held[1]]
    for i in range(2, 10):
        sums[i % 2] = sums[i % 2] + ended(i)
    live = lax.broadcasted_iota(jnp.int32, sums[0].shape, 0) < count_ref[0]
    out_ref[1] = jnp.where(live, sums[0], 0.0).astype(BF16)
    mix[0, 0] = sums[1]
    mix[0, 1] = ended(10) + ended(11)
    targets = [dest_ref[i] for i in range(ROWS)]
    for i in range(ROWS):
        rank = jnp.int32(0)
        for j in range(i):
            rank = rank + jnp.where(targets[j] == targets[i], 1, 0)
        column, away = lax.div(targets[i], 2), lax.rem(targets[i], 2)
        away = jnp.where(away == upper, 0, 1)
        row = lax.rem(x - column + nx, nx) * cap + jnp.minimum(rank, cap - 1)
        mix[1, 0, i : i + 1, :] = mix[0, away, pl.ds(row, 1), :]
    out_ref[0] = mix[1, 0].astype(BF16)
    for copy in started:
        copy.wait_send()


def per_device(
    image_slots, image_cot, text_rows, text_cot, destination, text_count, w_gate, w_up, w_down
):
    groups = lax.axis_size("group")
    nt, ndp = lax.axis_size("tp"), lax.axis_size("dp")
    nx, ny = groups // 2, ndp // 2
    slot_dev, feat = image_slots.shape
    hid = w_gate.shape[1]
    cap = slot_dev // groups
    half = nt // 4
    vm, dma = pltpu.VMEM, pltpu.SemaphoreType.DMA
    block = (KINDS, ROWS, feat)
    rows = (KINDS, PART, hid)
    hops = nt // 2
    span = half * KINDS * ROWS
    pair = (half, 2, ROWS, feat)
    scratch = [
        vm((feat, hid), BF16), vm((feat, hid), BF16), vm((hid, feat), BF16),
        vm((nx, 2, 2, cap, feat), BF16), vm((nx, 2, 2, cap, feat), BF16),
        vm((2, 2, ROWS, feat), F32), vm((nt, KINDS, 2, ROWS, feat), BF16),
        vm((4, span, feat), BF16), vm((4, span, feat), BF16),
        vm((4, 3, 2, ny, *rows), BF16), vm((4, 3, ny, *rows), BF16),
        vm((4, 3, ny, *rows), BF16), vm((4, 3, ny, *rows), BF16),
        vm((4, 2, ny, KINDS, PART, 2 * hid), BF16), vm((4, span, 2 * hid), BF16),
        vm((2, 2 * half, *block), BF16),
        vm(pair, BF16), vm(pair, BF16), vm(pair, BF16), vm(pair, BF16),
        vm((32, ROWS, feat), BF16), vm((32, ROWS, feat), BF16),
        vm((2, ROWS, feat), F32),
        dma((3,)), dma((nx,)), dma((nx,)), dma((12 * hops,)), dma((12 * hops,)),
        dma((12,)), dma((12,)), dma((12 * ny,)), dma((12 * ny,)), dma((4 * ny,)), dma((4 * ny,)),
        dma((4 * ny,)), dma((4 * ny,)), dma((2 * half,)), dma((2 * half,)),
        dma((32,)), dma((32,)),
    ]
    whole = pl.BlockSpec(memory_space=pltpu.VMEM)
    apart = pl.BlockSpec(memory_space=pl.ANY)
    scalars = pl.BlockSpec(memory_space=pltpu.SMEM)
    out = jax.ShapeDtypeStruct((2, ROWS, feat), BF16)
    grads = pl.pallas_call(
        functools.partial(kernel, nx, nt, ny, cap, feat, hid),
        out_shape=out,
        in_specs=[whole] * 4 + [scalars] * 2 + [apart] * 3,
        out_specs=whole,
        scratch_shapes=scratch,
        compiler_params=pltpu.CompilerParams(
            collective_id=0, has_side_effects=True, vmem_limit_bytes=VMEM_BYTES
        ),
    )(image_slots, image_cot, text_rows, text_cot, destination[:, 0], text_count,
      w_gate, w_up, w_down)
    return grads[0], grads[1]


def solution(mesh):
    placed = (
        P(("group", "tp"), "dp"),
        P(("group", "tp"), "dp"),
        P(("group", "tp"), "dp"),
        P(("group", "tp"), "dp"),
        P(("group", "tp"), None),
        P(("group", "tp")),
        P("dp", "tp"),
        P("dp", "tp"),
        P("tp", "dp"),
    )
    return jax.shard_map(
        per_device,
        mesh=mesh,
        in_specs=placed,
        out_specs=(P(("group", "tp"), "dp"), P(("group", "tp"), "dp")),
        check_vma=False,
    )
```
